128 devices in a mesh: wide: 8 (over y_lo, z), narrow: 16 (over y_hi, x, core).
Axes of the slice: x: 4, y: 4 (y_hi: 2, y_lo: 2; y = y_hi * 2 + y_lo), z: 4, core: 2. Of those that a mesh axis runs over, the one named last changes fastest.
Arguments:
- hidden: bfloat16 [1024, 4096], P('wide', 'narrow'), may hold values from -6 to 6
- norm_gain: float32 [4096], replicated, may hold values from 0.1 to 1.9
- w_query: bfloat16 [4096, 8192], P(None, 'narrow'), may hold values from -0.09375 to 0.09375
- w_keyval: bfloat16 [4096, 1024], P('narrow'), may hold values from -0.09375 to 0.09375
- query_gain: float32 [128], replicated, may hold values from 0.5 to 4
- key_gain: float32 [128], replicated, may hold values from 0.5 to 4
- cache_keys: bfloat16 [64, 16384, 512], P('wide', 'narrow'), may hold values from -300 to 300
- cache_values: bfloat16 [64, 16384, 512], P('wide', 'narrow'), may hold values from -6 to 6
- cache_lengths: int32 [64], P('wide'), may hold values from 1 to 16384
- owner_rank: int32 [64], P('wide'), may hold values from 0 to 7, as said below
- draft_mask: int32 [64, 16, 16], P('wide'), may hold values from 0 to 1, as said below
- w_output: bfloat16 [8192, 4096], P('narrow'), may hold values from -0.0625 to 0.0625
Outputs:
- projected: bfloat16 [1024, 4096], P('wide', 'narrow')
The draws below stay inside these ranges and needn't reach their ends.
Inputs may be any that keep to these rules, and one draw needn't show every extreme that they name: `owner_rank`: in each aligned block of 8 requests every index of wide is named exactly 1 times. Row t of a request marks the ancestors of draft token t in a tree of draft tokens and t itself: draft_mask[r, t, t] = 1 and draft_mask[r, t, u] = 0 for u > t.
All inputs are finite; a program needn't handle non-finite values.
Results may differ from the reference program's by a relative error of at most 0.007.
The reference program's roundings to bfloat16 on the way count: a program that leaves them out, or rounds other values in their place, can miss the bound.
Values may be sent and summed in bfloat16 or wider, within the bound.
No kernel may reach another device: no remote copies, remote signals or barrier semaphores. Data moves between devices by JAX's collectives and lax.ppermute only.
A program may use at most 192 MiB of HBM per device.

```python
import math
import jax
import jax.numpy as jnp
from jax import lax

D = 4096
HQ = 64
KVH = 4
HD = 128
DRAFT = 16
WIN = 16384
REQ_DEV = 8
REQS = 64
TOKENS = 1024
CAP = 1


def draw_cache_keys(key, part):
    normals = jax.random.normal(jax.random.fold_in(key, 11), (REQS, WIN, KVH * HD), jnp.float32) * 2.0
    return jnp.clip(normals, -300.0, 300.0).astype(jnp.bfloat16)


def draw_owner_rank(key, part):
    sources = REQS // REQ_DEV
    per_pair = REQ_DEV // sources

    def one_source(index):
        return jax.random.permutation(jax.random.fold_in(jax.random.fold_in(key, 21), index), REQ_DEV) // per_pair
    ranks = jax.vmap(one_source)(jnp.arange(sources, dtype=jnp.int32))
    return ranks.reshape(REQS).astype(jnp.int32)


def draw_draft_mask(key, part):

    def one_request(request_key):
        upper = jnp.maximum(jnp.arange(DRAFT, dtype=jnp.int32), 1)
        parents = jax.random.randint(request_key, (DRAFT,), 0, upper)
        identity = jnp.eye(DRAFT, dtype=jnp.int32)
        ancestry = identity
        for index in range(1, DRAFT):
            ancestry = ancestry.at[index].set(jnp.maximum(ancestry[parents[index]], identity[index]))
        return ancestry
    request_keys = jax.random.split(jax.random.fold_in(key, 31), REQS)
    return jax.vmap(one_request)(request_keys).astype(jnp.int32)


def set_ends(array, own_key, least, top_value):
    extent = array.shape
    place = [jax.random.randint(jax.random.fold_in(own_key, axis), (), 0, extent[axis]) for axis in range(len(extent))]
    array = array.at[tuple(place)].set(least)
    longest = extent.index(max(extent))
    place[longest] = (place[longest] + 1) % extent[longest]
    return array.at[tuple(place)].set(top_value)


def level_of(own_key, dims, cuts, low, largest):
    level, own = 1.0, jax.random.fold_in(own_key, 6)
    for position, shards_of in cuts:
        steps = jnp.exp(jax.random.uniform(jax.random.fold_in(own, position), (shards_of,), jnp.float32, low / len(cuts), largest / len(cuts)))
        level = level * jnp.repeat(steps, dims[position] // shards_of).reshape([-1 if axis == position else 1 for axis in range(len(dims))])
    return level


def bell_draw(stream_key, dims, spread, most, cuts=(), held_as=jnp.bfloat16):
    entries = spread * jax.random.normal(stream_key, dims, jnp.float32)
    if cuts:
        entries = entries * level_of(stream_key, dims, cuts, -0.22, 0.18)
    return jnp.clip(entries, -most, most).astype(held_as)


def setup_inputs(seed: int = 0) -> dict:
    key_of = jax.random.split(jax.random.key(seed), 13)
    hidden = bell_draw(key_of[0], (TOKENS, D), 1.0, 6.0, ((0, 8), (1, 16)))
    norm_gain = jnp.clip(1.0 + 0.18 * jax.random.normal(key_of[1], (D,), jnp.float32), 0.1, 1.9)
    w_query = bell_draw(key_of[2], (D, HQ * HD), D ** -0.5, 0.09375, ((1, 16),))
    w_keyval = bell_draw(key_of[3], (D, 2 * KVH * HD), D ** -0.5, 0.09375, ((0, 16),))
    query_gain = jnp.clip(jnp.exp(jax.random.uniform(key_of[4], (HD,), jnp.float32, math.log(0.5), math.log(4.0))), 0.5, 4.0)
    key_gain = jnp.clip(jnp.exp(jax.random.uniform(key_of[5], (HD,), jnp.float32, math.log(0.5), math.log(4.0))), 0.5, 4.0)
    cache_keys = draw_cache_keys(jax.random.fold_in(key_of[12], 71), 0)
    cache_values = bell_draw(key_of[7], (REQS, WIN, KVH * HD), 1.0, 6.0, ((0, 8), (1, 16)))
    cache_lengths = set_ends(jax.random.randint(key_of[8], (REQS,), 1, WIN + 1), jax.random.fold_in(key_of[8], 1), 1, WIN).astype(jnp.int32)
    owner_rank = draw_owner_rank(jax.random.fold_in(key_of[12], 71), 0)
    draft_mask = draw_draft_mask(jax.random.fold_in(key_of[12], 71), 0)
    w_output = bell_draw(key_of[11], (HQ * HD, D), (HQ * HD) ** -0.5, 0.0625, ((0, 16),))
    return {"hidden": hidden, "norm_gain": norm_gain, "w_query": w_query, "w_keyval": w_keyval, "query_gain": query_gain, "key_gain": key_gain, "cache_keys": cache_keys, "cache_values": cache_values, "cache_lengths": cache_lengths, "owner_rank": owner_rank, "draft_mask": draft_mask, "w_output": w_output}


epsilon = 1e-06
masked_fill = -1e+30

def rms_norm(values, gain_row):
    return values * lax.rsqrt(lax.optimization_barrier(jnp.mean(values * values, axis=-1, keepdims=True)) + epsilon) * gain_row

def reference(hidden, norm_gain, w_query, w_keyval, query_gain, key_gain, cache_keys, cache_values, cache_lengths, owner_rank, draft_mask, w_output):
    group = HQ // KVH
    inv_sqrt = 1.0 / math.sqrt(HD)
    normed = rms_norm(hidden.astype(jnp.float32), norm_gain.astype(jnp.float32)).astype(jnp.bfloat16)
    queries = jnp.dot(normed, w_query, preferred_element_type=jnp.float32).reshape(TOKENS, HQ, HD)
    queries = rms_norm(queries, query_gain.astype(jnp.float32)).astype(jnp.bfloat16)
    keyval = jnp.dot(normed, w_keyval, preferred_element_type=jnp.float32)
    new_keys = rms_norm(keyval[:, :KVH * HD].reshape(TOKENS, KVH, HD), key_gain.astype(jnp.float32)).astype(jnp.bfloat16)
    new_values = keyval[:, KVH * HD:].reshape(TOKENS, KVH, HD).astype(jnp.bfloat16)
    request_ids = jnp.arange(REQS, dtype=jnp.int32)
    source = request_ids // REQ_DEV
    earlier_same = (source[:, None] == source[None, :]) & (owner_rank[:, None] == owner_rank[None, :]) & (request_ids[None, :] < request_ids[:, None])
    rank_within = lax.optimization_barrier(jnp.sum(earlier_same.astype(jnp.int32), axis=1)).astype(jnp.int32)
    cache_slot = (owner_rank * REQ_DEV + source * CAP + rank_within).astype(jnp.int32)

    def attend(request_args):
        query_rows, key_rows, value_rows, slot_index, mask_rows = request_args
        cached_k = cache_keys[slot_index].reshape(WIN, KVH, HD).astype(jnp.float32)
        cached_v = cache_values[slot_index].reshape(WIN, KVH, HD).astype(jnp.float32)
        live_length = cache_lengths[slot_index]
        grouped = query_rows.reshape(DRAFT, KVH, group, HD).astype(jnp.float32)
        cache_scores = jnp.einsum('tkgd,skd->kgts', grouped, cached_k) * inv_sqrt
        live_keys = jnp.arange(WIN, dtype=jnp.int32) < live_length
        cache_scores = jnp.where(live_keys, cache_scores, masked_fill)
        draft_scores = jnp.einsum('tkgd,skd->kgts', grouped, key_rows.astype(jnp.float32)) * inv_sqrt
        allowed = mask_rows == 1
        draft_scores = jnp.where(allowed, draft_scores, masked_fill)
        maxima = jnp.maximum(lax.optimization_barrier(jnp.max(cache_scores, axis=-1)), lax.optimization_barrier(jnp.max(draft_scores, axis=-1)))[..., None]
        cache_weights = jnp.where(live_keys, jnp.exp(cache_scores - maxima), 0.0)
        draft_weights = jnp.where(allowed, jnp.exp(draft_scores - maxima), 0.0)
        totals = lax.optimization_barrier(jnp.sum(cache_weights, axis=-1)) + lax.optimization_barrier(jnp.sum(draft_weights, axis=-1))
        weighted = jnp.einsum('kgts,skd->kgtd', cache_weights.astype(jnp.bfloat16).astype(jnp.float32), cached_v)
        weighted = weighted + jnp.einsum('kgts,skd->kgtd', draft_weights.astype(jnp.bfloat16).astype(jnp.float32), value_rows.astype(jnp.float32))
        output = weighted / totals[..., None]
        return output.transpose(2, 0, 1, 3).reshape(DRAFT, HQ * HD).astype(jnp.bfloat16)
    attended = lax.map(attend, (queries.reshape(REQS, DRAFT, HQ, HD), new_keys.reshape(REQS, DRAFT, KVH, HD), new_values.reshape(REQS, DRAFT, KVH, HD), cache_slot, draft_mask))
    attended = attended.reshape(TOKENS, HQ * HD)
    return jnp.dot(attended, w_output, preferred_element_type=jnp.float32).astype(jnp.bfloat16)
```

```python
import math

import jax
import jax.numpy as jnp
from jax import lax
from jax.experimental import pallas as pl
from jax.experimental.pallas import tpu as pltpu
from jax.sharding import Mesh
from jax.sharding import PartitionSpec as P

HQ = 64
KVH = 4
HD = 128
DRAFT = 16
WIDE = 8
CHIPS = 8
CORES = 2
PER_HEAD = HQ // (CHIPS * CORES)
ROWS = PER_HEAD * DRAFT

EPS = 1e-06
DEAD = -1e30
LOG2E = 1.4426950408889634
SCALE2 = LOG2E / math.sqrt(HD)
F32 = jnp.float32
BF16 = jnp.bfloat16


def vmem():
    return pl.BlockSpec(memory_space=pltpu.VMEM)


def smem():
    return pl.BlockSpec(memory_space=pltpu.SMEM)


def rms(values, gain_row):
    mean = jnp.mean(values * values, axis=-1, keepdims=True)
    return values * lax.rsqrt(mean + EPS) * gain_row


def route_kernel(owner_ref, hidden_ref, mask_ref, out_ref):
    for r in range(WIDE):
        target = owner_ref[r]
        low = hidden_ref[r * DRAFT : (r + 1) * DRAFT, :HD]
        high = hidden_ref[r * DRAFT : (r + 1) * DRAFT, HD:]
        marks = mask_ref[r]
        for c in range(CHIPS):
            out_ref[target, c, 0:16, :] = low
            out_ref[target, c, 16:32, :] = high
            out_ref[target, c, 32:40, :] = marks


def features(ref, c):
    low = ref[:, c, 0:16, :].reshape(WIDE * DRAFT, HD)
    high = ref[:, c, 16:32, :].reshape(WIDE * DRAFT, HD)
    return jnp.concatenate([low, high], axis=1)


def query_kernel(own_ref, other_ref, gain_ref, wq_ref, wkv_ref, qgain_ref, out_ref):
    core = lax.axis_index("core")
    chip = lax.axis_index("chip")
    tokens = WIDE * DRAFT
    squares = jnp.zeros((tokens, 2 * HD), F32)
    for ref in (own_ref, other_ref):
        for c in range(CHIPS):
            block = features(ref, c).astype(F32)
            squares = squares + block * block
    width = CHIPS * CORES * 2 * HD
    scale = lax.rsqrt(jnp.sum(squares, axis=-1, keepdims=True) * (1.0 / width) + EPS)

    def normed(ref, c, side):
        block = features(ref, c).astype(F32)
        return (block * scale * gain_ref[c, pl.ds(side, 1), :]).astype(BF16)

    total = jnp.zeros((tokens, PER_HEAD * HD), F32)
    for c in range(CHIPS):
        for ref, side in ((own_ref, core), (other_ref, 1 - core)):
            total = total + jnp.dot(
                normed(ref, c, side), wq_ref[c, side], preferred_element_type=F32
            )
    for j in range(PER_HEAD):
        head = rms(total[:, j * HD : (j + 1) * HD], qgain_ref[...]).astype(BF16)
        head = head.reshape(WIDE, DRAFT, HD)
        for b in range(WIDE):
            start = b * ROWS + j * DRAFT
            for c in range(CHIPS):
                out_ref[c, start : start + DRAFT, :] = head[b]
    keyval = jnp.dot(normed(own_ref, chip, core), wkv_ref[...], preferred_element_type=F32)
    base = WIDE * ROWS
    for c in range(CHIPS):
        kv = c // (CHIPS // KVH)
        keys = keyval[:, kv * HD : (kv + 1) * HD]
        values = keyval[:, (KVH + kv) * HD : (KVH + kv + 1) * HD]
        out_ref[c, base : base + tokens, :] = keys.astype(BF16)
        out_ref[c, base + tokens : base + 2 * tokens, :] = values.astype(BF16)


def attend_kernel(
    length_ref, q_own_ref, q_other_ref, key_ref, value_ref, o_own_ref, o_other_ref, lse_ref
):
    b = pl.program_id(0)
    span = key_ref.shape[1]
    index = lax.axis_index("chip") * CORES + lax.axis_index("core")
    live = length_ref[b] - index * span

    def unit(kv, masked):
        q = jnp.concatenate(
            [q_own_ref[2 * kv], q_own_ref[2 * kv + 1], q_other_ref[2 * kv], q_other_ref[2 * kv + 1]],
            axis=0,
        )
        keys = key_ref[0, :, kv * HD : (kv + 1) * HD]
        values = value_ref[0, :, kv * HD : (kv + 1) * HD]
        scores = lax.dot_general(q, keys, (((1,), (1,)), ((), ())), preferred_element_type=F32)
        if masked:
            place = lax.broadcasted_iota(jnp.int32, (1, span), 1)
            scores = jnp.where(place < live, scores, DEAD)
        top = jnp.max(scores, axis=-1, keepdims=True)
        weights = jnp.exp2((scores - top) * SCALE2)
        den = jnp.sum(weights, axis=-1, keepdims=True)
        summed = jnp.dot(weights.astype(BF16), values, preferred_element_type=F32)
        out = (summed / den).astype(BF16)
        o_own_ref[2 * kv] = out[0 * ROWS : 1 * ROWS]
        o_own_ref[2 * kv + 1] = out[1 * ROWS : 2 * ROWS]
        o_other_ref[2 * kv] = out[2 * ROWS : 3 * ROWS]
        o_other_ref[2 * kv + 1] = out[3 * ROWS : 4 * ROWS]
        lse = top * SCALE2 + jnp.log2(den)
        rows = lax.broadcasted_iota(jnp.int32, (HD, HD), 0)
        lanes = lax.broadcasted_iota(jnp.int32, (HD, HD), 1)
        for side in range(2):
            column = jnp.broadcast_to(lse[side * HD : (side + 1) * HD], (HD, HD))
            line = jnp.sum(jnp.where(rows == lanes, column, 0.0), axis=0, keepdims=True)
            lse_ref[0, side * KVH + kv : side * KVH + kv + 1, :] = line

    @pl.when(live <= 0)
    def _():
        o_own_ref[...] = jnp.zeros(o_own_ref.shape, BF16)
        o_other_ref[...] = jnp.zeros(o_other_ref.shape, BF16)
        lse_ref[...] = jnp.full(lse_ref.shape, DEAD, F32)

    @pl.when(live >= span)
    def _():
        for kv in range(KVH):
            unit(kv, False)

    @pl.when(jnp.logical_and(live > 0, live < span))
    def _():
        for kv in range(KVH):
            unit(kv, True)


def join_kernel(mine_ref, theirs_ref, lse_ref, lse_in_ref, out_ref):
    one = lse_ref[:, 0:KVH, :].reshape(WIDE * KVH, HD)
    two = lse_in_ref[:, KVH : 2 * KVH, :].reshape(WIDE * KVH, HD)
    top = jnp.maximum(one, two)
    weight_one = jnp.exp2(one - top)
    weight_two = jnp.exp2(two - top)
    den = weight_one + weight_two
    lse = (top + jnp.log2(den)).reshape(WIDE, KVH, HD)
    shares = jnp.concatenate(
        [weight_one / den, weight_two / den, jnp.zeros((2 * WIDE * KVH, HD), F32)], axis=0
    )
    shares = shares.T
    for b in range(WIDE):
        for kv in range(KVH):
            j = b * KVH + kv
            col_one = shares[:, j : j + 1]
            col_two = shares[:, WIDE * KVH + j : WIDE * KVH + j + 1]
            for p in range(2):
                c = 2 * kv + p
                at = slice(b * ROWS, (b + 1) * ROWS)
                part = slice(p * ROWS, (p + 1) * ROWS)
                mixed = (
                    mine_ref[c, at, :].astype(F32) * col_one[part]
                    + theirs_ref[c, at, :].astype(F32) * col_two[part]
                )
                out_ref[c, at, :] = mixed.astype(BF16)
    lanes = lax.broadcasted_iota(jnp.int32, (WIDE, HD), 1)
    for kv in range(KVH):
        line = lse[:, kv, :]
        first = line.astype(BF16).astype(F32)
        rest = line - first
        second = rest.astype(BF16).astype(F32)
        third = (rest - second).astype(BF16).astype(F32)
        turned = [pltpu.roll(x, ROWS, 1) for x in (first, second, third)]
        for p in range(2):
            a = first if p == 0 else turned[0]
            m = turned[1] if p == 0 else second
            z = third if p == 0 else turned[2]
            base = WIDE * ROWS
            tail = jnp.concatenate(
                [jnp.where(lanes < ROWS, a, m), jnp.where(lanes < ROWS, z, 0.0)], axis=0
            )
            out_ref[2 * kv + p, base : base + 2 * WIDE, :] = tail.astype(BF16)


def finish_kernel(
    part_ref, q_ref, kv_own_ref, kv_other_ref, kgain_ref, mask_ref, wo_ref, out_own_ref, out_other_ref
):
    core = lax.axis_index("core")
    tokens = WIDE * DRAFT
    base = WIDE * ROWS
    keys = jnp.zeros((tokens, HD), F32)
    values = jnp.zeros((tokens, HD), F32)
    for ref in (kv_own_ref, kv_other_ref):
        for c in range(CHIPS):
            keys = keys + ref[c, 0:tokens, :].astype(F32)
            values = values + ref[c, tokens : 2 * tokens, :].astype(F32)
    keys = rms(keys, kgain_ref[...]).astype(BF16)
    values = values.astype(BF16)

    lines = []
    for c in range(CHIPS):
        head = part_ref[c, base : base + WIDE, :].astype(F32)
        tail = part_ref[c, base + WIDE : base + 2 * WIDE, :].astype(F32)
        lines.append(head + pltpu.roll(head, ROWS, 1) + tail)
    lines = jnp.concatenate(lines + [jnp.zeros((HD - CHIPS * WIDE, HD), F32)], axis=0)
    columns = lines.T

    attended = []
    for b in range(WIDE):
        at = slice(b * ROWS, (b + 1) * ROWS)
        marks = mask_ref[b, 0].astype(F32)
        late = pltpu.roll(marks, HD - DRAFT, 1)
        lanes = lax.broadcasted_iota(jnp.int32, (DRAFT, HD), 1)
        marks = jnp.concatenate([marks, late], axis=0)
        marks = jnp.where(lanes < DRAFT, marks, 0.0)
        if b:
            marks = pltpu.roll(marks, b * DRAFT, 1)
        allowed = jnp.concatenate([marks] * PER_HEAD, axis=0) > 0.5
        scores = lax.dot_general(
            q_ref[0, at, :], keys, (((1,), (1,)), ((), ())), preferred_element_type=F32
        )
        scores = jnp.where(allowed, scores, DEAD)
        top = jnp.max(scores, axis=-1, keepdims=True)
        weights = jnp.exp2((scores - top) * SCALE2)
        den = jnp.sum(weights, axis=-1, keepdims=True)
        summed = jnp.dot(weights.astype(BF16), values, preferred_element_type=F32)
        cols = [columns[0:ROWS, c * WIDE + b : c * WIDE + b + 1] for c in range(CHIPS)]
        draft = top * SCALE2
        peak = draft
        for col in cols:
            peak = jnp.maximum(peak, col)
        share = jnp.exp2(draft - peak)
        numer = summed * share
        denom = den * share
        for c in range(CHIPS):
            share = jnp.exp2(cols[c] - peak)
            numer = numer + part_ref[c, at, :].astype(F32) * share
            denom = denom + share
        attended.append((numer / denom).astype(BF16))
    attended = jnp.stack(attended, axis=0)
    rows = jnp.concatenate(
        [
            attended[:, j * DRAFT : (j + 1) * DRAFT, :].reshape(tokens, HD)
            for j in range(PER_HEAD)
        ],
        axis=1,
    )
    piece = 2 * HD
    for c in range(CHIPS):
        for ref, side in ((out_own_ref, core), (out_other_ref, 1 - core)):
            column = pl.multiple_of((c * CORES + side) * piece, piece)
            out = jnp.dot(rows, wo_ref[:, pl.ds(column, piece)], preferred_element_type=F32)
            ref[:, c] = out.astype(BF16).reshape(WIDE, DRAFT, piece)


def pair_kernel(one_ref, two_ref, out_ref):
    out_ref[...] = (one_ref[...].astype(F32) + two_ref[...].astype(F32)).astype(BF16)


def gather_kernel(owner_ref, part_ref, out_ref):
    for r in range(WIDE):
        source = owner_ref[r]
        total = part_ref[source, 0].astype(F32)
        for c in range(1, CHIPS):
            total = total + part_ref[source, c].astype(F32)
        out_ref[r * DRAFT : (r + 1) * DRAFT, :] = total.astype(BF16)


def swap(x):
    return lax.ppermute(x, "core", [(0, 1), (1, 0)])


def exchange(x, axes):
    return lax.all_to_all(x, axes, split_axis=0, concat_axis=0, tiled=True)


def local(
    hidden,
    norm_gain,
    w_query,
    w_keyval,
    query_gain,
    key_gain,
    cache_keys,
    cache_values,
    cache_lengths,
    owner_rank,
    draft_mask,
    w_output,
):
    chip = lax.axis_index("chip")
    tokens = WIDE * DRAFT
    piece = 2 * HD
    span = cache_keys.shape[1]
    shape = jax.ShapeDtypeStruct

    marks = draft_mask.astype(BF16)
    marks = jnp.concatenate(
        [marks[:, :8], marks[:, 8:], jnp.zeros((WIDE, 8, HD - 2 * DRAFT), BF16)], axis=2
    )
    sent = pl.pallas_call(
        route_kernel,
        out_shape=shape((WIDE, CHIPS, 40, HD), BF16),
        in_specs=[smem(), vmem(), vmem()],
        out_specs=vmem(),
    )(owner_rank, hidden, marks)
    arrived = exchange(sent.reshape(WIDE * CHIPS, 40, HD), ("wide", "chip"))
    partner = swap(arrived)
    arrived = arrived.reshape(WIDE, CHIPS, 40, HD)
    partner = partner.reshape(WIDE, CHIPS, 40, HD)

    extended = WIDE * ROWS + 2 * tokens
    queries = pl.pallas_call(
        query_kernel,
        out_shape=shape((CHIPS, extended, HD), BF16),
        in_specs=[vmem()] * 6,
        out_specs=vmem(),
    )(
        arrived,
        partner,
        norm_gain.reshape(CHIPS, CORES, piece),
        w_query.reshape(CHIPS, CORES, piece, PER_HEAD * HD),
        w_keyval,
        query_gain.reshape(1, HD),
    )
    q_own = exchange(queries, "chip")
    q_other = swap(q_own)

    q_spec = pl.BlockSpec((CHIPS, ROWS, HD), lambda b: (0, b, 0))
    kv_spec = pl.BlockSpec((1, span, KVH * HD), lambda b: (b, 0, 0))
    o_own, o_other, lse = pl.pallas_call(
        attend_kernel,
        out_shape=(
            shape((CHIPS, WIDE * ROWS, HD), BF16),
            shape((CHIPS, WIDE * ROWS, HD), BF16),
            shape((WIDE, 2 * KVH, HD), F32),
        ),
        grid=(WIDE,),
        in_specs=[smem(), q_spec, q_spec, kv_spec, kv_spec],
        out_specs=(q_spec, q_spec, pl.BlockSpec((1, 2 * KVH, HD), lambda b: (b, 0, 0))),
    )(cache_lengths, q_own, q_other, cache_keys, cache_values)

    theirs = swap(o_other)
    lse_in = swap(lse)
    joined = pl.pallas_call(
        join_kernel,
        out_shape=shape((CHIPS, WIDE * ROWS + 2 * WIDE, HD), BF16),
        in_specs=[vmem()] * 4,
        out_specs=vmem(),
    )(o_own, theirs, lse, lse_in)
    parts = exchange(joined, "chip")

    kv_spec = pl.BlockSpec((CHIPS, 2 * tokens, HD), lambda i: (0, WIDE * ROWS // (2 * tokens), 0))
    full = lambda *dims: pl.BlockSpec(dims, lambda i: (0,) * len(dims))
    out_own, out_other = pl.pallas_call(
        finish_kernel,
        out_shape=(shape((WIDE, CHIPS, DRAFT, piece), BF16),) * 2,
        grid=(1,),
        in_specs=[
            full(CHIPS, WIDE * ROWS + 2 * WIDE, HD),
            full(1, WIDE * ROWS, HD),
            kv_spec,
            kv_spec,
            full(1, HD),
            pl.BlockSpec((WIDE, 1, 8, HD), lambda i: (0, 0, 4, 0)),
            full(PER_HEAD * HD, w_output.shape[1]),
        ],
        out_specs=(full(WIDE, CHIPS, DRAFT, piece),) * 2,
    )(parts, queries, q_own, q_other, key_gain.reshape(1, HD), arrived, w_output)

    summed = pl.pallas_call(
        pair_kernel,
        out_shape=shape((WIDE, CHIPS, DRAFT, piece), BF16),
        in_specs=[vmem()] * 2,
        out_specs=vmem(),
    )(out_own, swap(out_other))
    back = exchange(summed.reshape(WIDE * CHIPS, DRAFT, piece), ("wide", "chip"))
    return pl.pallas_call(
        gather_kernel,
        out_shape=shape((tokens, piece), BF16),
        in_specs=[smem(), vmem()],
        out_specs=vmem(),
    )(owner_rank, back.reshape(WIDE, CHIPS, DRAFT, piece))


def solution(mesh):
    fine = Mesh(mesh.devices.reshape(WIDE, CHIPS, CORES), ("wide", "chip", "core"))
    narrow = ("chip", "core")
    in_specs = (
        P("wide", narrow),
        P(),
        P(None, narrow),
        P(narrow, None),
        P(),
        P(),
        P("wide", narrow, None),
        P("wide", narrow, None),
        P("wide"),
        P("wide"),
        P("wide", None, None),
        P(narrow, None),
    )
    out_specs = P("wide", narrow)
    return jax.shard_map(local, mesh=fine, in_specs=in_specs, out_specs=out_specs, check_vma=False)
```

```python
import math

import jax
import jax.numpy as jnp
from jax import lax
from jax.experimental import pallas as pl
from jax.experimental.pallas import tpu as pltpu
from jax.sharding import Mesh
from jax.sharding import PartitionSpec as P

HQ = 64
KVH = 4
HD = 128
DRAFT = 16
WIDE = 8
CHIPS = 8
CORES = 2
PER_HEAD = HQ // (CHIPS * CORES)
ROWS = PER_HEAD * DRAFT

EPS = 1e-06
DEAD = -1e30
LOG2E = 1.4426950408889634
SCALE2 = LOG2E / math.sqrt(HD)
F32 = jnp.float32
BF16 = jnp.bfloat16


def vmem():
    return pl.BlockSpec(memory_space=pltpu.VMEM)


def smem():
    return pl.BlockSpec(memory_space=pltpu.SMEM)


def rms(values, gain_row):
    mean = jnp.mean(values * values, axis=-1, keepdims=True)
    return values * lax.rsqrt(mean + EPS) * gain_row


def route_kernel(owner_ref, hidden_ref, mask_ref, out_ref):
    for r in range(WIDE):
        target = owner_ref[r]
        low = hidden_ref[r * DRAFT : (r + 1) * DRAFT, :HD]
        high = hidden_ref[r * DRAFT : (r + 1) * DRAFT, HD:]
        marks = mask_ref[r]
        for c in range(CHIPS):
            out_ref[target, c, 0:16, :] = low
            out_ref[target, c, 16:32, :] = high
            out_ref[target, c, 32:40, :] = marks


def features(ref, c):
    low = ref[:, c, 0:16, :].reshape(WIDE * DRAFT, HD)
    high = ref[:, c, 16:32, :].reshape(WIDE * DRAFT, HD)
    return jnp.concatenate([low, high], axis=1)


def query_kernel(own_ref, other_ref, gain_ref, wq_ref, wkv_ref, qgain_ref, out_ref):
    core = lax.axis_index("core")
    chip = lax.axis_index("chip")
    tokens = WIDE * DRAFT
    squares = jnp.zeros((tokens, 2 * HD), F32)
    for ref in (own_ref, other_ref):
        for c in range(CHIPS):
            block = features(ref, c).astype(F32)
            squares = squares + block * block
    width = CHIPS * CORES * 2 * HD
    scale = lax.rsqrt(jnp.sum(squares, axis=-1, keepdims=True) * (1.0 / width) + EPS)

    def normed(ref, c, side):
        block = features(ref, c).astype(F32)
        return (block * scale * gain_ref[c, pl.ds(side, 1), :]).astype(BF16)

    total = jnp.zeros((tokens, PER_HEAD * HD), F32)
    for c in range(CHIPS):
        for ref, side in ((own_ref, core), (other_ref, 1 - core)):
            total = total + jnp.dot(
                normed(ref, c, side), wq_ref[c, side], preferred_element_type=F32
            )
    for j in range(PER_HEAD):
        head = rms(total[:, j * HD : (j + 1) * HD], qgain_ref[...]).astype(BF16)
        head = head.reshape(WIDE, DRAFT, HD)
        for b in range(WIDE):
            start = b * ROWS + j * DRAFT
            for c in range(CHIPS):
                out_ref[c, start : start + DRAFT, :] = head[b]
    keyval = jnp.dot(normed(own_ref, chip, core), wkv_ref[...], preferred_element_type=F32)
    base = WIDE * ROWS
    for c in range(CHIPS):
        kv = c // (CHIPS // KVH)
        keys = keyval[:, kv * HD : (kv + 1) * HD]
        values = keyval[:, (KVH + kv) * HD : (KVH + kv + 1) * HD]
        out_ref[c, base : base + tokens, :] = keys.astype(BF16)
        out_ref[c, base + tokens : base + 2 * tokens, :] = values.astype(BF16)


def attend_kernel(
    length_ref, q_own_ref, q_other_ref, key_ref, value_ref, o_own_ref, o_other_ref, lse_ref
):
    b = pl.program_id(0)
    span = key_ref.shape[1]
    index = lax.axis_index("chip") * CORES + lax.axis_index("core")
    live = length_ref[b] - index * span

    def unit(kv, masked):
        q = jnp.concatenate(
            [q_own_ref[2 * kv], q_own_ref[2 * kv + 1], q_other_ref[2 * kv], q_other_ref[2 * kv + 1]],
            axis=0,
        )
        keys = key_ref[0, :, kv * HD : (kv + 1) * HD]
        values = value_ref[0, :, kv * HD : (kv + 1) * HD]
        scores = lax.dot_general(q, keys, (((1,), (1,)), ((), ())), preferred_element_type=F32)
        if masked:
            place = lax.broadcasted_iota(jnp.int32, (1, span), 1)
            scores = jnp.where(place < live, scores, DEAD)
        top = jnp.max(scores, axis=-1, keepdims=True)
        weights = jnp.exp2((scores - top) * SCALE2)
        den = jnp.sum(weights, axis=-1, keepdims=True)
        summed = jnp.dot(weights.astype(BF16), values, preferred_element_type=F32)
        out = (summed / den).astype(BF16)
        o_own_ref[2 * kv] = out[0 * ROWS : 1 * ROWS]
        o_own_ref[2 * kv + 1] = out[1 * ROWS : 2 * ROWS]
        o_other_ref[2 * kv] = out[2 * ROWS : 3 * ROWS]
        o_other_ref[2 * kv + 1] = out[3 * ROWS : 4 * ROWS]
        lse = top * SCALE2 + jnp.log2(den)
        rows = lax.broadcasted_iota(jnp.int32, (HD, HD), 0)
        lanes = lax.broadcasted_iota(jnp.int32, (HD, HD), 1)
        for side in range(2):
            column = jnp.broadcast_to(lse[side * HD : (side + 1) * HD], (HD, HD))
            line = jnp.sum(jnp.where(rows == lanes, column, 0.0), axis=0, keepdims=True)
            lse_ref[0, side * KVH + kv : side * KVH + kv + 1, :] = line

    @pl.when(live <= 0)
    def _():
        o_own_ref[...] = jnp.zeros(o_own_ref.shape, BF16)
        o_other_ref[...] = jnp.zeros(o_other_ref.shape, BF16)
        lse_ref[...] = jnp.full(lse_ref.shape, DEAD, F32)

    @pl.when(live >= span)
    def _():
        for kv in range(KVH):
            unit(kv, False)

    @pl.when(jnp.logical_and(live > 0, live < span))
    def _():
        for kv in range(KVH):
            unit(kv, True)


def join_kernel(mine_ref, theirs_ref, lse_ref, lse_in_ref, out_ref):
    one = lse_ref[:, 0:KVH, :].reshape(WIDE * KVH, HD)
    two = lse_in_ref[:, KVH : 2 * KVH, :].reshape(WIDE * KVH, HD)
    top = jnp.maximum(one, two)
    weight_one = jnp.exp2(one - top)
    weight_two = jnp.exp2(two - top)
    den = weight_one + weight_two
    lse = (top + jnp.log2(den)).reshape(WIDE, KVH, HD)
    shares = jnp.concatenate(
        [weight_one / den, weight_two / den, jnp.zeros((2 * WIDE * KVH, HD), F32)], axis=0
    )
    shares = shares.T
    for b in range(WIDE):
        for kv in range(KVH):
            j = b * KVH + kv
            col_one = shares[:, j : j + 1]
            col_two = shares[:, WIDE * KVH + j : WIDE * KVH + j + 1]
            for p in range(2):
                c = 2 * kv + p
                at = slice(b * ROWS, (b + 1) * ROWS)
                part = slice(p * ROWS, (p + 1) * ROWS)
                mixed = (
                    mine_ref[c, at, :].astype(F32) * col_one[part]
                    + theirs_ref[c, at, :].astype(F32) * col_two[part]
                )
                out_ref[c, at, :] = mixed.astype(BF16)
    lanes = lax.broadcasted_iota(jnp.int32, (WIDE, HD), 1)
    for kv in range(KVH):
        line = lse[:, kv, :]
        first = line.astype(BF16).astype(F32)
        rest = line - first
        second = rest.astype(BF16).astype(F32)
        third = (rest - second).astype(BF16).astype(F32)
        turned = [pltpu.roll(x, ROWS, 1) for x in (first, second, third)]
        for p in range(2):
            a = first if p == 0 else turned[0]
            m = turned[1] if p == 0 else second
            z = third if p == 0 else turned[2]
            base = WIDE * ROWS
            tail = jnp.concatenate(
                [jnp.where(lanes < ROWS, a, m), jnp.where(lanes < ROWS, z, 0.0)], axis=0
            )
            out_ref[2 * kv + p, base : base + 2 * WIDE, :] = tail.astype(BF16)


def finish_kernel(
    part_ref, q_ref, kv_own_ref, kv_other_ref, kgain_ref, mask_ref, wo_ref, out_own_ref, out_other_ref
):
    core = lax.axis_index("core")
    tokens = WIDE * DRAFT
    base = WIDE * ROWS
    keys = jnp.zeros((tokens, HD), F32)
    values = jnp.zeros((tokens, HD), F32)
    for ref in (kv_own_ref, kv_other_ref):
        for c in range(CHIPS):
            keys = keys + ref[c, 0:tokens, :].astype(F32)
            values = values + ref[c, tokens : 2 * tokens, :].astype(F32)
    keys = rms(keys, kgain_ref[...]).astype(BF16)
    values = values.astype(BF16)

    lines = []
    for c in range(CHIPS):
        head = part_ref[c, base : base + WIDE, :].astype(F32)
        tail = part_ref[c, base + WIDE : base + 2 * WIDE, :].astype(F32)
        lines.append(head + pltpu.roll(head, ROWS, 1) + tail)
    lines = jnp.concatenate(lines + [jnp.zeros((HD - CHIPS * WIDE, HD), F32)], axis=0)
    columns = lines.T

    attended = []
    for b in range(WIDE):
        at = slice(b * ROWS, (b + 1) * ROWS)
        marks = mask_ref[b, 0].astype(F32)
        late = pltpu.roll(marks, HD - DRAFT, 1)
        lanes = lax.broadcasted_iota(jnp.int32, (DRAFT, HD), 1)
        marks = jnp.concatenate([marks, late], axis=0)
        marks = jnp.where(lanes < DRAFT, marks, 0.0)
        if b:
            marks = pltpu.roll(marks, b * DRAFT, 1)
        allowed = jnp.concatenate([marks] * PER_HEAD, axis=0) > 0.5
        scores = lax.dot_general(
            q_ref[0, at, :], keys, (((1,), (1,)), ((), ())), preferred_element_type=F32
        )
        scores = jnp.where(allowed, scores, DEAD)
        top = jnp.max(scores, axis=-1, keepdims=True)
        weights = jnp.exp2((scores - top) * SCALE2)
        den = jnp.sum(weights, axis=-1, keepdims=True)
        summed = jnp.dot(weights.astype(BF16), values, preferred_element_type=F32)
        cols = [columns[0:ROWS, c * WIDE + b : c * WIDE + b + 1] for c in range(CHIPS)]
        draft = top * SCALE2
        peak = draft
        for col in cols:
            peak = jnp.maximum(peak, col)
        share = jnp.exp2(draft - peak)
        numer = summed * share
        denom = den * share
        for c in range(CHIPS):
            share = jnp.exp2(cols[c] - peak)
            numer = numer + part_ref[c, at, :].astype(F32) * share
            denom = denom + share
        attended.append((numer / denom).astype(BF16))
    attended = jnp.stack(attended, axis=0)
    rows = jnp.concatenate(
        [
            attended[:, j * DRAFT : (j + 1) * DRAFT, :].reshape(tokens, HD)
            for j in range(PER_HEAD)
        ],
        axis=1,
    )
    piece = 2 * HD
    for c in range(CHIPS):
        for ref, side in ((out_own_ref, core), (out_other_ref, 1 - core)):
            column = pl.multiple_of((c * CORES + side) * piece, piece)
            out = jnp.dot(rows, wo_ref[:, pl.ds(column, piece)], preferred_element_type=F32)
            ref[:, c] = out.astype(BF16).reshape(WIDE, DRAFT, piece)


def pair_kernel(one_ref, two_ref, out_ref):
    out_ref[...] = (one_ref[...].astype(F32) + two_ref[...].astype(F32)).astype(BF16)


def gather_kernel(owner_ref, part_ref, out_ref):
    for r in range(WIDE):
        source = owner_ref[r]
        total = part_ref[source, 0].astype(F32)
        for c in range(1, CHIPS):
            total = total + part_ref[source, c].astype(F32)
        out_ref[r * DRAFT : (r + 1) * DRAFT, :] = total.astype(BF16)


def swap(x):
    return lax.ppermute(x, "core", [(0, 1), (1, 0)])


def exchange(x, axes):
    return lax.all_to_all(x, axes, split_axis=0, concat_axis=0, tiled=True)


def local(
    hidden,
    norm_gain,
    w_query,
    w_keyval,
    query_gain,
    key_gain,
    cache_keys,
    cache_values,
    cache_lengths,
    owner_rank,
    draft_mask,
    w_output,
):
    chip = lax.axis_index("chip")
    tokens = WIDE * DRAFT
    piece = 2 * HD
    span = cache_keys.shape[1]
    shape = jax.ShapeDtypeStruct

    marks = draft_mask.astype(BF16)
    marks = jnp.concatenate(
        [marks[:, :8], marks[:, 8:], jnp.zeros((WIDE, 8, HD - 2 * DRAFT), BF16)], axis=2
    )
    sent = pl.pallas_call(
        route_kernel,
        compiler_params=pltpu.CompilerParams(vmem_limit_bytes=4 * 1024 * 1024),
        out_shape=shape((WIDE, CHIPS, 40, HD), BF16),
        in_specs=[smem(), vmem(), vmem()],
        out_specs=vmem(),
    )(owner_rank, hidden, marks)
    arrived = exchange(sent.reshape(WIDE * CHIPS, 40, HD), ("wide", "chip"))
    partner = swap(arrived)
    arrived = arrived.reshape(WIDE, CHIPS, 40, HD)
    partner = partner.reshape(WIDE, CHIPS, 40, HD)

    extended = WIDE * ROWS + 2 * tokens
    queries = pl.pallas_call(
        query_kernel,
        compiler_params=pltpu.CompilerParams(vmem_limit_bytes=16 * 1024 * 1024),
        out_shape=shape((CHIPS, extended, HD), BF16),
        in_specs=[vmem()] * 6,
        out_specs=vmem(),
    )(
        arrived,
        partner,
        norm_gain.reshape(CHIPS, CORES, piece),
        w_query.reshape(CHIPS, CORES, piece, PER_HEAD * HD),
        w_keyval,
        query_gain.reshape(1, HD),
    )
    q_own = exchange(queries, "chip")
    q_other = swap(q_own)

    q_spec = pl.BlockSpec((CHIPS, ROWS, HD), lambda b: (0, b, 0))
    kv_spec = pl.BlockSpec((1, span, KVH * HD), lambda b: (b, 0, 0))
    o_own, o_other, lse = pl.pallas_call(
        attend_kernel,
        compiler_params=pltpu.CompilerParams(vmem_limit_bytes=16 * 1024 * 1024),
        out_shape=(
            shape((CHIPS, WIDE * ROWS, HD), BF16),
            shape((CHIPS, WIDE * ROWS, HD), BF16),
            shape((WIDE, 2 * KVH, HD), F32),
        ),
        grid=(WIDE,),
        in_specs=[smem(), q_spec, q_spec, kv_spec, kv_spec],
        out_specs=(q_spec, q_spec, pl.BlockSpec((1, 2 * KVH, HD), lambda b: (b, 0, 0))),
    )(
        cache_lengths,
        q_own,
        q_other,
        pltpu.with_memory_space_constraint(cache_keys, pltpu.HBM),
        pltpu.with_memory_space_constraint(cache_values, pltpu.HBM),
    )

    theirs = swap(o_other)
    lse_in = swap(lse)
    joined = pl.pallas_call(
        join_kernel,
        compiler_params=pltpu.CompilerParams(vmem_limit_bytes=8 * 1024 * 1024),
        out_shape=shape((CHIPS, WIDE * ROWS + 2 * WIDE, HD), BF16),
        in_specs=[vmem()] * 4,
        out_specs=vmem(),
    )(o_own, theirs, lse, lse_in)
    parts = exchange(joined, "chip")

    kv_spec = pl.BlockSpec((CHIPS, 2 * tokens, HD), lambda i: (0, WIDE * ROWS // (2 * tokens), 0))
    full = lambda *dims: pl.BlockSpec(dims, lambda i: (0,) * len(dims))
    out_own, out_other = pl.pallas_call(
        finish_kernel,
        compiler_params=pltpu.CompilerParams(vmem_limit_bytes=16 * 1024 * 1024),
        out_shape=(shape((WIDE, CHIPS, DRAFT, piece), BF16),) * 2,
        grid=(1,),
        in_specs=[
            full(CHIPS, WIDE * ROWS + 2 * WIDE, HD),
            full(1, WIDE * ROWS, HD),
            kv_spec,
            kv_spec,
            full(1, HD),
            pl.BlockSpec((WIDE, 1, 8, HD), lambda i: (0, 0, 4, 0)),
            full(PER_HEAD * HD, w_output.shape[1]),
        ],
        out_specs=(full(WIDE, CHIPS, DRAFT, piece),) * 2,
    )(parts, queries, q_own, q_other, key_gain.reshape(1, HD), arrived, w_output)

    summed = pl.pallas_call(
        pair_kernel,
        compiler_params=pltpu.CompilerParams(vmem_limit_bytes=4 * 1024 * 1024),
        out_shape=shape((WIDE, CHIPS, DRAFT, piece), BF16),
        in_specs=[vmem()] * 2,
        out_specs=vmem(),
    )(out_own, swap(out_other))
    back = exchange(summed.reshape(WIDE * CHIPS, DRAFT, piece), ("wide", "chip"))
    return pl.pallas_call(
        gather_kernel,
        compiler_params=pltpu.CompilerParams(vmem_limit_bytes=4 * 1024 * 1024),
        out_shape=shape((tokens, piece), BF16),
        in_specs=[smem(), vmem()],
        out_specs=vmem(),
    )(owner_rank, back.reshape(WIDE, CHIPS, DRAFT, piece))


def solution(mesh):
    fine = Mesh(mesh.devices.reshape(WIDE, CHIPS, CORES), ("wide", "chip", "core"))
    narrow = ("chip", "core")
    in_specs = (
        P("wide", narrow),
        P(),
        P(None, narrow),
        P(narrow, None),
        P(),
        P(),
        P("wide", narrow, None),
        P("wide", narrow, None),
        P("wide"),
        P("wide"),
        P("wide", None, None),
        P(narrow, None),
    )
    out_specs = P("wide", narrow)
    return jax.shard_map(local, mesh=fine, in_specs=in_specs, out_specs=out_specs, check_vma=False)
```

```python
import functools
import math

import jax
import jax.numpy as jnp
from jax import lax
from jax.experimental import pallas as pl
from jax.experimental.pallas import tpu as pltpu
from jax.sharding import Mesh
from jax.sharding import PartitionSpec as P

HQ = 64
KVH = 4
HD = 128
DRAFT = 16
WIDE = 8
CHIPS = 8
CORES = 2
PER_HEAD = HQ // (CHIPS * CORES)
ROWS = PER_HEAD * DRAFT

EPS = 1e-06
DEAD = -1e30
LOG2E = 1.4426950408889634
SCALE2 = LOG2E / math.sqrt(HD)
F32 = jnp.float32
BF16 = jnp.bfloat16


def vmem():
    return pl.BlockSpec(memory_space=pltpu.VMEM)


def smem():
    return pl.BlockSpec(memory_space=pltpu.SMEM)


def anywhere():
    return pl.BlockSpec(memory_space=pl.ANY)


def rms(values, gain_row):
    mean = jnp.mean(values * values, axis=-1, keepdims=True)
    return values * lax.rsqrt(mean + EPS) * gain_row


def route_kernel(owner_ref, hidden_ref, mask_ref, out_ref):
    blank = jnp.zeros((DRAFT // 2, HD - 2 * DRAFT), F32)
    for r in range(WIDE):
        target = owner_ref[r]
        low = hidden_ref[r * DRAFT : (r + 1) * DRAFT, :HD]
        high = hidden_ref[r * DRAFT : (r + 1) * DRAFT, HD:]
        marks = mask_ref[r].astype(F32)
        marks = jnp.concatenate([marks[: DRAFT // 2], marks[DRAFT // 2 :], blank], axis=1)
        marks = marks.astype(BF16)
        for c in range(CHIPS):
            out_ref[target, c, 0:16, :] = low
            out_ref[target, c, 16:32, :] = high
            out_ref[target, c, 32:40, :] = marks


def features(ref, c):
    low = ref[:, c, 0:16, :].reshape(WIDE * DRAFT, HD)
    high = ref[:, c, 16:32, :].reshape(WIDE * DRAFT, HD)
    return jnp.concatenate([low, high], axis=1)


def query_kernel(
    own_ref,
    other_ref,
    gain_far,
    wq_far,
    wkv_far,
    qgain_far,
    out_ref,
    kv_ref,
    mine_ref,
    marks_ref,
    gain_ref,
    wq_ref,
    wkv_ref,
    qgain_ref,
    sem,
):
    gain_copy = pltpu.make_async_copy(gain_far, gain_ref, sem.at[0])
    qgain_copy = pltpu.make_async_copy(qgain_far, qgain_ref, sem.at[1])
    wkv_copy = pltpu.make_async_copy(wkv_far, wkv_ref, sem.at[2])
    wq_copies = [
        pltpu.make_async_copy(wq_far.at[c], wq_ref.at[c], sem.at[3 + c]) for c in range(CHIPS)
    ]
    for copy in [gain_copy, qgain_copy] + wq_copies + [wkv_copy]:
        copy.start()
    core = lax.axis_index("core")
    chip = lax.axis_index("chip")
    tokens = WIDE * DRAFT
    squares = jnp.zeros((tokens, 2 * HD), F32)
    for ref in (own_ref, other_ref):
        for c in range(CHIPS):
            block = features(ref, c).astype(F32)
            squares = squares + block * block
    width = CHIPS * CORES * 2 * HD
    scale = lax.rsqrt(jnp.sum(squares, axis=-1, keepdims=True) * (1.0 / width) + EPS)

    def normed(ref, c, side):
        block = features(ref, c).astype(F32)
        gain = gain_ref[pl.ds((c * CORES + side) * 2, 2), :]
        gain = jnp.concatenate([gain[0:1], gain[1:2]], axis=1)
        return (block * scale * gain).astype(BF16)

    gain_copy.wait()
    total = jnp.zeros((tokens, PER_HEAD * HD), F32)
    for c in range(CHIPS):
        wq_copies[c].wait()
        for ref, side in ((own_ref, core), (other_ref, 1 - core)):
            total = total + jnp.dot(
                normed(ref, c, side), wq_ref[c, side], preferred_element_type=F32
            )
    qgain_copy.wait()
    for j in range(PER_HEAD):
        head = rms(total[:, j * HD : (j + 1) * HD], qgain_ref[...]).astype(BF16)
        head = head.reshape(WIDE, DRAFT, HD)
        for b in range(WIDE):
            start = b * ROWS + j * DRAFT
            mine_ref[start : start + DRAFT, :] = head[b]
            for c in range(CHIPS):
                out_ref[c, start : start + DRAFT, :] = head[b]
    for b in range(WIDE):
        marks_ref[b] = own_ref[b, 0, 32:40, :]
    wkv_copy.wait()
    keyval = jnp.dot(normed(own_ref, chip, core), wkv_ref[...], preferred_element_type=F32)
    for c in range(CHIPS):
        kv = c // (CHIPS // KVH)
        keys = keyval[:, kv * HD : (kv + 1) * HD]
        values = keyval[:, (KVH + kv) * HD : (KVH + kv + 1) * HD]
        kv_ref[c, 0:tokens, :] = keys.astype(BF16)
        kv_ref[c, tokens : 2 * tokens, :] = values.astype(BF16)


def attend_kernel(
    first, length_ref, q_own_ref, q_other_ref, key_ref, value_ref, o_own_ref, o_other_ref, lse_ref,
    s_ref, p_ref, m_ref,
):
    b = pl.program_id(0)
    span = key_ref.shape[1]
    tile = 2 * HD
    tiles = span // tile
    index = lax.axis_index("chip") * CORES + lax.axis_index("core")
    live = length_ref[first + b] - index * span
    ones = jnp.ones((span, HD), BF16)
    rows = lax.broadcasted_iota(jnp.int32, (HD, HD), 0)
    lanes = lax.broadcasted_iota(jnp.int32, (HD, HD), 1)

    def query(kv):
        return jnp.concatenate(
            [q_own_ref[2 * kv], q_own_ref[2 * kv + 1], q_other_ref[2 * kv], q_other_ref[2 * kv + 1]],
            axis=0,
        )

    def score(kv, i, q, top, masked):
        at = slice(i * tile, (i + 1) * tile)
        keys = key_ref[0, at, kv * HD : (kv + 1) * HD]
        part = lax.dot_general(q, keys, (((1,), (1,)), ((), ())), preferred_element_type=F32)
        if masked:
            place = lax.broadcasted_iota(jnp.int32, (1, tile), 1) + i * tile
            part = jnp.where(place < live, part, DEAD)
        s_ref[kv % 2, :, at] = part
        high = jnp.maximum(part[:, :HD], part[:, HD:])
        return high if top is None else jnp.maximum(top, high)

    def close(kv, top):
        m_ref[kv % 2] = jnp.broadcast_to(jnp.max(top, axis=-1, keepdims=True), top.shape)

    def soft(kv, i):
        count = KVH * ROWS // tiles
        at = slice(i * count, (i + 1) * count)
        top = m_ref[kv % 2, at, :]
        for j in range(span // HD):
            part = s_ref[kv % 2, at, j * HD : (j + 1) * HD]
            p_ref[kv % 2, at, j * HD : (j + 1) * HD] = jnp.exp2((part - top) * SCALE2).astype(BF16)

    def value(kv):
        values = jnp.concatenate([value_ref[0, :, kv * HD : (kv + 1) * HD], ones], axis=1)
        summed = jnp.dot(p_ref[kv % 2], values, preferred_element_type=F32)
        den = summed[:, HD:]
        out = (summed[:, :HD] / den).astype(BF16)
        o_own_ref[2 * kv] = out[0 * ROWS : 1 * ROWS]
        o_own_ref[2 * kv + 1] = out[1 * ROWS : 2 * ROWS]
        o_other_ref[2 * kv] = out[2 * ROWS : 3 * ROWS]
        o_other_ref[2 * kv + 1] = out[3 * ROWS : 4 * ROWS]
        lse = m_ref[kv % 2] * SCALE2 + jnp.log2(den)
        for side in range(2):
            block = lse[side * HD : (side + 1) * HD]
            line = jnp.sum(jnp.where(rows == lanes, block, 0.0), axis=0, keepdims=True)
            lse_ref[0, side * KVH + kv : side * KVH + kv + 1, :] = line

    def whole(masked):
        for stage in range(KVH + 1):
            top = None
            q = query(stage) if stage < KVH else None
            for i in range(tiles):
                if stage < KVH:
                    top = score(stage, i, q, top, masked)
                if stage > 0:
                    soft(stage - 1, i)
            if stage > 0:
                value(stage - 1)
            if stage < KVH:
                close(stage, top)

    @pl.when(live <= 0)
    def _():
        o_own_ref[...] = jnp.zeros(o_own_ref.shape, BF16)
        o_other_ref[...] = jnp.zeros(o_other_ref.shape, BF16)
        lse_ref[...] = jnp.full(lse_ref.shape, DEAD, F32)

    @pl.when(live >= span)
    def _():
        whole(False)

    @pl.when(jnp.logical_and(live > 0, live < span))
    def _():
        whole(True)


def join_kernel(
    mine_ref, theirs_ref, lse_ref, lse_in_ref, kv_own_ref, kv_other_ref, out_ref, kv_ref
):
    one = lse_ref[:, 0:KVH, :].reshape(WIDE * KVH, HD)
    two = lse_in_ref[:, KVH : 2 * KVH, :].reshape(WIDE * KVH, HD)
    top = jnp.maximum(one, two)
    weight_one = jnp.exp2(one - top)
    weight_two = jnp.exp2(two - top)
    den = weight_one + weight_two
    lse = (top + jnp.log2(den)).reshape(WIDE, KVH, HD)
    shares = jnp.concatenate(
        [weight_one / den, weight_two / den, jnp.zeros((2 * WIDE * KVH, HD), F32)], axis=0
    )
    shares = shares.T
    for b in range(WIDE):
        for kv in range(KVH):
            j = b * KVH + kv
            col_one = shares[:, j : j + 1]
            col_two = shares[:, WIDE * KVH + j : WIDE * KVH + j + 1]
            for p in range(2):
                c = 2 * kv + p
                at = slice(b * ROWS, (b + 1) * ROWS)
                part = slice(p * ROWS, (p + 1) * ROWS)
                mixed = (
                    mine_ref[c, at, :].astype(F32) * col_one[part]
                    + theirs_ref[c, at, :].astype(F32) * col_two[part]
                )
                out_ref[c, at, :] = mixed.astype(BF16)
    lanes = lax.broadcasted_iota(jnp.int32, (WIDE, HD), 1)
    for kv in range(KVH):
        line = lse[:, kv, :]
        first = line.astype(BF16).astype(F32)
        rest = line - first
        second = rest.astype(BF16).astype(F32)
        third = (rest - second).astype(BF16).astype(F32)
        turned = [pltpu.roll(x, ROWS, 1) for x in (first, second, third)]
        for p in range(2):
            a = first if p == 0 else turned[0]
            m = turned[1] if p == 0 else second
            z = third if p == 0 else turned[2]
            base = WIDE * ROWS
            tail = jnp.concatenate(
                [jnp.where(lanes < ROWS, a, m), jnp.where(lanes < ROWS, z, 0.0)], axis=0
            )
            out_ref[2 * kv + p, base : base + 2 * WIDE, :] = tail.astype(BF16)
    total = jnp.zeros(kv_ref.shape, F32)
    for ref in (kv_own_ref, kv_other_ref):
        for c in range(CHIPS):
            total = total + ref[c].astype(F32)
    kv_ref[...] = total


def draft_kernel(q_ref, kv_ref, kgain_ref, mask_ref, out_ref, lse_ref):
    tokens = WIDE * DRAFT
    keys = rms(kv_ref[0:tokens, :], kgain_ref[...]).astype(BF16)
    values = kv_ref[tokens : 2 * tokens, :].astype(BF16)
    lanes = lax.broadcasted_iota(jnp.int32, (DRAFT, HD), 1)
    for b in range(WIDE):
        at = slice(b * ROWS, (b + 1) * ROWS)
        marks = mask_ref[b].astype(F32)
        late = pltpu.roll(marks, HD - DRAFT, 1)
        marks = jnp.concatenate([marks, late], axis=0)
        marks = jnp.where(lanes < DRAFT, marks, 0.0)
        if b:
            marks = pltpu.roll(marks, b * DRAFT, 1)
        allowed = jnp.concatenate([marks] * PER_HEAD, axis=0) > 0.5
        scores = lax.dot_general(
            q_ref[at, :], keys, (((1,), (1,)), ((), ())), preferred_element_type=F32
        )
        scores = jnp.where(allowed, scores, DEAD)
        top = jnp.max(scores, axis=-1, keepdims=True)
        weights = jnp.exp2((scores - top) * SCALE2)
        den = jnp.sum(weights, axis=-1, keepdims=True)
        summed = jnp.dot(weights.astype(BF16), values, preferred_element_type=F32)
        out_ref[at, :] = summed / den
        lse_ref[at, :] = jnp.broadcast_to(top * SCALE2 + jnp.log2(den), (ROWS, HD))


def finish_kernel(
    part_ref, draft_ref, lse_ref, wo_far, out_own_ref, out_other_ref, wo_ref, sem
):
    core = lax.axis_index("core")
    tokens = WIDE * DRAFT
    wo_copies = []
    for c in range(CHIPS):
        columns = pl.ds(c * CORES * 2 * HD, CORES * 2 * HD)
        wo_copies.append(
            pltpu.make_async_copy(wo_far.at[:, columns], wo_ref.at[:, columns], sem.at[c])
        )
        wo_copies[c].start()
    base = WIDE * ROWS
    lines = []
    for c in range(CHIPS):
        head = part_ref[c, base : base + WIDE, :].astype(F32)
        tail = part_ref[c, base + WIDE : base + 2 * WIDE, :].astype(F32)
        lines.append(head + pltpu.roll(head, ROWS, 1) + tail)
    columns = jnp.concatenate(lines + [jnp.zeros((HD - CHIPS * WIDE, HD), F32)], axis=0).T
    attended = []
    for b in range(WIDE):
        at = slice(b * ROWS, (b + 1) * ROWS)
        cols = [columns[0:ROWS, c * WIDE + b : c * WIDE + b + 1] for c in range(CHIPS)]
        cols = [jnp.broadcast_to(col, (ROWS, HD)) for col in cols]
        draft = lse_ref[at, :]
        peak = draft
        for col in cols:
            peak = jnp.maximum(peak, col)
        share = jnp.exp2(draft - peak)
        numer = draft_ref[at, :] * share
        denom = share
        for c in range(CHIPS):
            share = jnp.exp2(cols[c] - peak)
            numer = numer + part_ref[c, at, :].astype(F32) * share
            denom = denom + share
        attended.append((numer / denom).astype(BF16))
    attended = jnp.stack(attended, axis=0)
    rows = jnp.concatenate(
        [
            attended[:, j * DRAFT : (j + 1) * DRAFT, :].reshape(tokens, HD)
            for j in range(PER_HEAD)
        ],
        axis=1,
    )
    piece = 2 * HD
    for c in range(CHIPS):
        wo_copies[c].wait()
        for ref, side in ((out_own_ref, core), (out_other_ref, 1 - core)):
            column = pl.multiple_of((c * CORES + side) * piece, piece)
            out = jnp.dot(rows, wo_ref[:, pl.ds(column, piece)], preferred_element_type=F32)
            ref[:, c] = out.astype(BF16).reshape(WIDE, DRAFT, piece)


def pair_kernel(one_ref, two_ref, out_ref):
    out_ref[...] = (one_ref[...].astype(F32) + two_ref[...].astype(F32)).astype(BF16)


def gather_kernel(owner_ref, part_ref, out_ref):
    for r in range(WIDE):
        source = owner_ref[r]
        total = part_ref[source, 0].astype(F32)
        for c in range(1, CHIPS):
            total = total + part_ref[source, c].astype(F32)
        out_ref[r * DRAFT : (r + 1) * DRAFT, :] = total.astype(BF16)


def swap(x):
    return lax.ppermute(x, "core", [(0, 1), (1, 0)])


def exchange(x, axes):
    return lax.all_to_all(x, axes, split_axis=0, concat_axis=0, tiled=True)


def local(
    hidden,
    norm_gain,
    w_query,
    w_keyval,
    query_gain,
    key_gain,
    cache_keys,
    cache_values,
    cache_lengths,
    owner_rank,
    draft_mask,
    w_output,
):
    tokens = WIDE * DRAFT
    piece = 2 * HD
    span = cache_keys.shape[1]
    shape = jax.ShapeDtypeStruct

    far = lambda x: pltpu.with_memory_space_constraint(x, pltpu.HBM)
    sent = pl.pallas_call(
        route_kernel,
        compiler_params=pltpu.CompilerParams(vmem_limit_bytes=4 * 1024 * 1024),
        out_shape=shape((WIDE, CHIPS, 40, HD), BF16),
        in_specs=[smem(), vmem(), vmem()],
        out_specs=vmem(),
    )(far(owner_rank), far(hidden), far(draft_mask))
    arrived = exchange(sent.reshape(WIDE * CHIPS, 40, HD), ("wide", "chip"))
    partner = swap(arrived)
    arrived = arrived.reshape(WIDE, CHIPS, 40, HD)
    partner = partner.reshape(WIDE, CHIPS, 40, HD)

    queries, keyval, mine, marks = pl.pallas_call(
        query_kernel,
        compiler_params=pltpu.CompilerParams(vmem_limit_bytes=16 * 1024 * 1024),
        out_shape=(
            shape((CHIPS, WIDE * ROWS, HD), BF16),
            shape((CHIPS, 2 * tokens, HD), BF16),
            shape((WIDE * ROWS, HD), BF16),
            shape((WIDE, DRAFT // 2, HD), BF16),
        ),
        in_specs=[vmem()] * 2 + [anywhere()] * 4,
        out_specs=(vmem(),) * 4,
        scratch_shapes=[
            pltpu.VMEM((CHIPS * CORES * 2, HD), F32),
            pltpu.VMEM((CHIPS, CORES, piece, PER_HEAD * HD), BF16),
            pltpu.VMEM((piece, 2 * KVH * HD), BF16),
            pltpu.VMEM((1, HD), F32),
            pltpu.SemaphoreType.DMA((3 + CHIPS,)),
        ],
    )(
        arrived,
        partner,
        far(norm_gain.reshape(CHIPS * CORES * 2, HD)),
        far(w_query.reshape(CHIPS, CORES, piece, PER_HEAD * HD)),
        far(w_keyval),
        far(query_gain.reshape(1, HD)),
    )
    q_own = exchange(queries, "chip")
    q_own, keyval = lax.optimization_barrier((q_own, keyval))
    kv_own = exchange(keyval, "chip")
    q_other = swap(q_own)

    q_spec = pl.BlockSpec((CHIPS, ROWS, HD), lambda b: (0, b, 0))
    kv_spec = pl.BlockSpec((1, span, KVH * HD), lambda b: (b, 0, 0))
    attend = pl.pallas_call(
        functools.partial(attend_kernel, 0),
        cost_estimate=pl.CostEstimate(
            flops=8 * WIDE * KVH * KVH * ROWS * span * HD,
            bytes_accessed=4 * WIDE * span * KVH * HD,
            transcendentals=WIDE * KVH * KVH * ROWS * span,
        ),
        compiler_params=pltpu.CompilerParams(vmem_limit_bytes=16 * 1024 * 1024),
        scratch_shapes=[
            pltpu.VMEM((2, KVH * ROWS, span), F32),
            pltpu.VMEM((2, KVH * ROWS, span), BF16),
            pltpu.VMEM((2, KVH * ROWS, HD), F32),
        ],
        out_shape=(
            shape((CHIPS, WIDE * ROWS, HD), BF16),
            shape((CHIPS, WIDE * ROWS, HD), BF16),
            shape((WIDE, 2 * KVH, HD), F32),
        ),
        grid=(WIDE,),
        in_specs=[smem(), q_spec, q_spec, kv_spec, kv_spec],
        out_specs=(q_spec, q_spec, pl.BlockSpec((1, 2 * KVH, HD), lambda b: (b, 0, 0))),
    )
    o_own, o_other, lse = attend(
        cache_lengths, q_own, far(q_other), far(cache_keys), far(cache_values)
    )

    kv_other = swap(kv_own)
    joined, keyval = pl.pallas_call(
        join_kernel,
        compiler_params=pltpu.CompilerParams(vmem_limit_bytes=8 * 1024 * 1024),
        out_shape=(
            shape((CHIPS, WIDE * ROWS + 2 * WIDE, HD), BF16),
            shape((2 * tokens, HD), F32),
        ),
        in_specs=[vmem()] * 6,
        out_specs=(vmem(), vmem()),
    )(o_own, swap(o_other), lse, swap(lse), kv_own, kv_other)
    parts = exchange(joined, "chip")

    drafted, draft_lse = pl.pallas_call(
        draft_kernel,
        compiler_params=pltpu.CompilerParams(vmem_limit_bytes=8 * 1024 * 1024),
        cost_estimate=pl.CostEstimate(
            flops=4000000000, bytes_accessed=2000000, transcendentals=70000
        ),
        out_shape=(shape((WIDE * ROWS, HD), F32),) * 2,
        in_specs=[vmem()] * 4,
        out_specs=(vmem(), vmem()),
    )(mine, keyval, key_gain.reshape(1, HD), marks)

    out_own, out_other = pl.pallas_call(
        finish_kernel,
        compiler_params=pltpu.CompilerParams(vmem_limit_bytes=16 * 1024 * 1024),
        out_shape=(shape((WIDE, CHIPS, DRAFT, piece), BF16),) * 2,
        in_specs=[vmem()] * 3 + [anywhere()],
        out_specs=(vmem(), vmem()),
        scratch_shapes=[
            pltpu.VMEM(w_output.shape, BF16),
            pltpu.SemaphoreType.DMA((CHIPS,)),
        ],
    )(parts, drafted, draft_lse, far(w_output))

    summed = pl.pallas_call(
        pair_kernel,
        compiler_params=pltpu.CompilerParams(vmem_limit_bytes=4 * 1024 * 1024),
        out_shape=shape((WIDE, CHIPS, DRAFT, piece), BF16),
        in_specs=[vmem()] * 2,
        out_specs=vmem(),
    )(out_own, swap(out_other))
    back = exchange(summed.reshape(WIDE * CHIPS, DRAFT, piece), ("wide", "chip"))
    return pl.pallas_call(
        gather_kernel,
        compiler_params=pltpu.CompilerParams(vmem_limit_bytes=4 * 1024 * 1024),
        out_shape=shape((tokens, piece), BF16),
        in_specs=[smem(), vmem()],
        out_specs=vmem(),
    )(owner_rank, back.reshape(WIDE, CHIPS, DRAFT, piece))


def solution(mesh):
    fine = Mesh(mesh.devices.reshape(WIDE, CHIPS, CORES), ("wide", "chip", "core"))
    narrow = ("chip", "core")
    in_specs = (
        P("wide", narrow),
        P(),
        P(None, narrow),
        P(narrow, None),
        P(),
        P(),
        P("wide", narrow, None),
        P("wide", narrow, None),
        P("wide"),
        P("wide"),
        P("wide", None, None),
        P(narrow, None),
    )
    out_specs = P("wide", narrow)

    return jax.shard_map(local, mesh=fine, in_specs=in_specs, out_specs=out_specs, check_vma=False)
```

```python
import math

import jax
import jax.numpy as jnp
from jax import lax
from jax.experimental import pallas as pl
from jax.experimental.pallas import tpu as pltpu
from jax.sharding import Mesh
from jax.sharding import PartitionSpec as P

HQ = 64
KVH = 4
HD = 128
DRAFT = 16
WIDE = 8
CHIPS = 8
CORES = 2
PER_HEAD = HQ // (CHIPS * CORES)
ROWS = PER_HEAD * DRAFT

EPS = 1e-06
DEAD = -1e30
LOG2E = 1.4426950408889634
SCALE2 = LOG2E / math.sqrt(HD)
F32 = jnp.float32
BF16 = jnp.bfloat16


def vmem():
    return pl.BlockSpec(memory_space=pltpu.VMEM)


def smem():
    return pl.BlockSpec(memory_space=pltpu.SMEM)


def anywhere():
    return pl.BlockSpec(memory_space=pl.ANY)


def rms(values, gain_row):
    mean = jnp.mean(values * values, axis=-1, keepdims=True)
    return values * lax.rsqrt(mean + EPS) * gain_row


def route_kernel(owner_ref, hidden_ref, mask_ref, out_ref):
    blank = jnp.zeros((DRAFT // 2, HD - 2 * DRAFT), F32)
    for r in range(WIDE):
        target = owner_ref[r]
        low = hidden_ref[r * DRAFT : (r + 1) * DRAFT, :HD]
        high = hidden_ref[r * DRAFT : (r + 1) * DRAFT, HD:]
        marks = mask_ref[r].astype(F32)
        marks = jnp.concatenate([marks[: DRAFT // 2], marks[DRAFT // 2 :], blank], axis=1)
        marks = marks.astype(BF16)
        for c in range(CHIPS):
            out_ref[target, c, 0:16, :] = low
            out_ref[target, c, 16:32, :] = high
            out_ref[target, c, 32:40, :] = marks


def features(ref, c):
    low = ref[:, c, 0:16, :].reshape(WIDE * DRAFT, HD)
    high = ref[:, c, 16:32, :].reshape(WIDE * DRAFT, HD)
    return jnp.concatenate([low, high], axis=1)


def query_kernel(
    own_ref,
    other_ref,
    gain_far,
    wq_far,
    qgain_far,
    mine_ref,
    slice_ref,
    marks_ref,
    gain_ref,
    wq_ref,
    qgain_ref,
    sem,
):
    gain_copy = pltpu.make_async_copy(gain_far, gain_ref, sem.at[0])
    qgain_copy = pltpu.make_async_copy(qgain_far, qgain_ref, sem.at[1])
    wq_copies = [
        pltpu.make_async_copy(wq_far.at[c], wq_ref.at[c], sem.at[2 + c]) for c in range(CHIPS)
    ]
    for copy in [gain_copy, qgain_copy] + wq_copies:
        copy.start()
    core = lax.axis_index("core")
    chip = lax.axis_index("chip")
    tokens = WIDE * DRAFT
    squares = jnp.zeros((tokens, 2 * HD), F32)
    for ref in (own_ref, other_ref):
        for c in range(CHIPS):
            block = features(ref, c).astype(F32)
            squares = squares + block * block
    width = CHIPS * CORES * 2 * HD
    scale = lax.rsqrt(jnp.sum(squares, axis=-1, keepdims=True) * (1.0 / width) + EPS)

    def normed(ref, c, side):
        block = features(ref, c).astype(F32)
        gain = gain_ref[pl.ds((c * CORES + side) * 2, 2), :]
        gain = jnp.concatenate([gain[0:1], gain[1:2]], axis=1)
        return (block * scale * gain).astype(BF16)

    gain_copy.wait()
    total = jnp.zeros((tokens, PER_HEAD * HD), F32)
    for c in range(CHIPS):
        wq_copies[c].wait()
        for ref, side in ((own_ref, core), (other_ref, 1 - core)):
            total = total + jnp.dot(
                normed(ref, c, side), wq_ref[c, side], preferred_element_type=F32
            )
    qgain_copy.wait()
    for j in range(PER_HEAD):
        head = rms(total[:, j * HD : (j + 1) * HD], qgain_ref[...]).astype(BF16)
        head = head.reshape(WIDE, DRAFT, HD)
        for b in range(WIDE):
            start = b * ROWS + j * DRAFT
            mine_ref[start : start + DRAFT, :] = head[b]
    for b in range(WIDE):
        marks_ref[b] = own_ref[b, 0, 32:40, :]
    slice_ref[...] = normed(own_ref, chip, core)


def keyval_kernel(slice_ref, wkv_ref, kv_ref):
    tokens = WIDE * DRAFT
    keyval = jnp.dot(slice_ref[...], wkv_ref[...], preferred_element_type=F32).astype(BF16)
    for c in range(CHIPS):
        kv = c // (CHIPS // KVH)
        kv_ref[c, 0:tokens, :] = keyval[:, kv * HD : (kv + 1) * HD]
        kv_ref[c, tokens : 2 * tokens, :] = keyval[:, (KVH + kv) * HD : (KVH + kv + 1) * HD]


def attend_kernel(length_ref, *refs):
    q_refs, refs = refs[: CHIPS * CORES], refs[CHIPS * CORES :]
    key_ref, value_ref, o_own_ref, o_other_ref, lse_ref, s_ref, p_ref, m_ref = refs
    b = pl.program_id(0)
    chip = lax.axis_index("chip")
    odd = lax.rem(chip, 2)
    span = key_ref.shape[1]
    tile = 2 * HD
    tiles = span // tile
    index = chip * CORES + lax.axis_index("core")
    live = length_ref[b] - index * span
    ones = jnp.ones((span, HD), BF16)
    rows = lax.broadcasted_iota(jnp.int32, (HD, HD), 0)
    lanes = lax.broadcasted_iota(jnp.int32, (HD, HD), 1)

    def head(kv):
        return jnp.bitwise_xor(chip // 2, kv)

    def columns(kv):
        return pl.ds(pl.multiple_of(head(kv) * HD, HD), HD)

    def query(kv):
        picked = [2 * kv, 2 * kv + 1, CHIPS + 2 * kv, CHIPS + 2 * kv + 1]
        here = pl.ds(pl.multiple_of(b * ROWS, ROWS), ROWS)
        return jnp.concatenate([q_refs[i][here, :] for i in picked], axis=0)

    def score(kv, i, q, top, masked):
        at = slice(i * tile, (i + 1) * tile)
        keys = key_ref[0, at, columns(kv)]
        part = lax.dot_general(q, keys, (((1,), (1,)), ((), ())), preferred_element_type=F32)
        if masked:
            place = lax.broadcasted_iota(jnp.int32, (1, tile), 1) + i * tile
            part = jnp.where(place < live, part, DEAD)
        s_ref[kv % 2, :, at] = part
        high = jnp.maximum(part[:, :HD], part[:, HD:])
        return high if top is None else jnp.maximum(top, high)

    def close(kv, top):
        m_ref[kv] = jnp.broadcast_to(jnp.max(top, axis=-1, keepdims=True), top.shape)

    def soft(kv, i):
        count = KVH * ROWS // tiles
        at = slice(i * count, (i + 1) * count)
        top = m_ref[kv, at, :]
        for j in range(span // HD):
            part = s_ref[kv % 2, at, j * HD : (j + 1) * HD]
            p_ref[kv % 2, at, j * HD : (j + 1) * HD] = jnp.exp2((part - top) * SCALE2).astype(BF16)

    def value(kv):
        values = jnp.concatenate([value_ref[0, :, columns(kv)], ones], axis=1)
        summed = jnp.dot(p_ref[kv % 2], values, preferred_element_type=F32)
        den = summed[:, HD:]
        out = (summed[:, :HD] / den).astype(BF16)
        for i in range(2):
            target = jnp.bitwise_xor(chip, 2 * kv + i)
            o_own_ref[target] = out[i * ROWS : (i + 1) * ROWS]
            o_other_ref[target] = out[(2 + i) * ROWS : (3 + i) * ROWS]
        lse = m_ref[kv] * SCALE2 + jnp.log2(den)
        for side in range(2):
            block = lse[side * HD : (side + 1) * HD]
            line = jnp.sum(jnp.where(rows == lanes, block, 0.0), axis=0, keepdims=True)
            line = jnp.where(odd == 1, pltpu.roll(line, ROWS, 1), line)
            lse_ref[0, pl.ds(side * KVH + head(kv), 1), :] = line

    def whole(masked):
        for stage in range(KVH + 2):
            top = None
            q = query(stage) if stage < KVH else None
            if stage > 1:
                value(stage - 2)
            for i in range(tiles):
                if stage < KVH:
                    top = score(stage, i, q, top, masked)
                if 0 < stage <= KVH:
                    soft(stage - 1, i)
            if stage < KVH:
                close(stage, top)

    @pl.when(live <= 0)
    def _():
        o_own_ref[...] = jnp.zeros(o_own_ref.shape, BF16)
        o_other_ref[...] = jnp.zeros(o_other_ref.shape, BF16)
        lse_ref[...] = jnp.full(lse_ref.shape, DEAD, F32)

    @pl.when(live >= span)
    def _():
        whole(False)

    @pl.when(jnp.logical_and(live > 0, live < span))
    def _():
        whole(True)


def join_kernel(mine_ref, theirs_ref, lse_ref, lse_in_ref, out_ref):
    one = lse_ref[:, 0:KVH, :].reshape(WIDE * KVH, HD)
    two = lse_in_ref[:, KVH : 2 * KVH, :].reshape(WIDE * KVH, HD)
    top = jnp.maximum(one, two)
    weight_one = jnp.exp2(one - top)
    weight_two = jnp.exp2(two - top)
    den = weight_one + weight_two
    lse = (top + jnp.log2(den)).reshape(WIDE, KVH, HD)
    shares = jnp.concatenate(
        [weight_one / den, weight_two / den, jnp.zeros((2 * WIDE * KVH, HD), F32)], axis=0
    )
    shares = shares.T
    for b in range(WIDE):
        for kv in range(KVH):
            j = b * KVH + kv
            col_one = shares[:, j : j + 1]
            col_two = shares[:, WIDE * KVH + j : WIDE * KVH + j + 1]
            for p in range(2):
                c = 2 * kv + p
                at = slice(b * ROWS, (b + 1) * ROWS)
                part = slice(p * ROWS, (p + 1) * ROWS)
                mixed = (
                    mine_ref[c, at, :].astype(F32) * col_one[part]
                    + theirs_ref[c, at, :].astype(F32) * col_two[part]
                )
                out_ref[c, at, :] = mixed.astype(BF16)
    lanes = lax.broadcasted_iota(jnp.int32, (WIDE, HD), 1)
    for kv in range(KVH):
        line = lse[:, kv, :]
        first = line.astype(BF16).astype(F32)
        rest = line - first
        second = rest.astype(BF16).astype(F32)
        third = (rest - second).astype(BF16).astype(F32)
        turned = [pltpu.roll(x, ROWS, 1) for x in (first, second, third)]
        for p in range(2):
            a = first if p == 0 else turned[0]
            m = turned[1] if p == 0 else second
            z = third if p == 0 else turned[2]
            base = WIDE * ROWS
            tail = jnp.concatenate(
                [jnp.where(lanes < ROWS, a, m), jnp.where(lanes < ROWS, z, 0.0)], axis=0
            )
            out_ref[2 * kv + p, base : base + 2 * WIDE, :] = tail.astype(BF16)


def draft_kernel(q_ref, kv_own_ref, kv_other_ref, kgain_ref, mask_ref, out_ref, lse_ref):
    tokens = WIDE * DRAFT
    total = jnp.zeros((2 * tokens, HD), F32)
    for ref in (kv_own_ref, kv_other_ref):
        for c in range(CHIPS):
            total = total + ref[c].astype(F32)
    keys = rms(total[:tokens], kgain_ref[...]).astype(BF16)
    values = total[tokens:].astype(BF16)
    lanes = lax.broadcasted_iota(jnp.int32, (DRAFT, HD), 1)
    for b in range(WIDE):
        at = slice(b * ROWS, (b + 1) * ROWS)
        marks = mask_ref[b].astype(F32)
        late = pltpu.roll(marks, HD - DRAFT, 1)
        marks = jnp.concatenate([marks, late], axis=0)
        marks = jnp.where(lanes < DRAFT, marks, 0.0)
        if b:
            marks = pltpu.roll(marks, b * DRAFT, 1)
        allowed = jnp.concatenate([marks] * PER_HEAD, axis=0) > 0.5
        scores = lax.dot_general(
            q_ref[at, :], keys, (((1,), (1,)), ((), ())), preferred_element_type=F32
        )
        scores = jnp.where(allowed, scores, DEAD)
        top = jnp.max(scores, axis=-1, keepdims=True)
        weights = jnp.exp2((scores - top) * SCALE2)
        den = jnp.sum(weights, axis=-1, keepdims=True)
        summed = jnp.dot(weights.astype(BF16), values, preferred_element_type=F32)
        out_ref[at, :] = summed / den
        lse_ref[at, :] = jnp.broadcast_to(top * SCALE2 + jnp.log2(den), (ROWS, HD))


def finish_kernel(
    part_ref, draft_ref, lse_ref, wo_far, out_own_ref, out_other_ref, wo_ref, sem
):
    core = lax.axis_index("core")
    tokens = WIDE * DRAFT
    wo_copies = []
    for c in range(CHIPS):
        columns = pl.ds(c * CORES * 2 * HD, CORES * 2 * HD)
        wo_copies.append(
            pltpu.make_async_copy(wo_far.at[:, columns], wo_ref.at[:, columns], sem.at[c])
        )
        wo_copies[c].start()
    base = WIDE * ROWS
    lines = []
    for c in range(CHIPS):
        head = part_ref[c, base : base + WIDE, :].astype(F32)
        tail = part_ref[c, base + WIDE : base + 2 * WIDE, :].astype(F32)
        lines.append(head + pltpu.roll(head, ROWS, 1) + tail)
    columns = jnp.concatenate(lines + [jnp.zeros((HD - CHIPS * WIDE, HD), F32)], axis=0).T
    attended = []
    for b in range(WIDE):
        at = slice(b * ROWS, (b + 1) * ROWS)
        cols = [columns[0:ROWS, c * WIDE + b : c * WIDE + b + 1] for c in range(CHIPS)]
        cols = [jnp.broadcast_to(col, (ROWS, HD)) for col in cols]
        draft = lse_ref[at, :]
        peak = draft
        for col in cols:
            peak = jnp.maximum(peak, col)
        share = jnp.exp2(draft - peak)
        numer = draft_ref[at, :] * share
        denom = share
        for c in range(CHIPS):
            share = jnp.exp2(cols[c] - peak)
            numer = numer + part_ref[c, at, :].astype(F32) * share
            denom = denom + share
        attended.append((numer / denom).astype(BF16))
    attended = jnp.stack(attended, axis=0)
    rows = jnp.concatenate(
        [
            attended[:, j * DRAFT : (j + 1) * DRAFT, :].reshape(tokens, HD)
            for j in range(PER_HEAD)
        ],
        axis=1,
    )
    piece = 2 * HD
    for c in range(CHIPS):
        wo_copies[c].wait()
        for ref, side in ((out_own_ref, core), (out_other_ref, 1 - core)):
            column = pl.multiple_of((c * CORES + side) * piece, piece)
            out = jnp.dot(rows, wo_ref[:, pl.ds(column, piece)], preferred_element_type=F32)
            ref[:, c] = out.astype(BF16).reshape(WIDE, DRAFT, piece)


def pair_kernel(one_ref, two_ref, out_ref):
    out_ref[...] = (one_ref[...].astype(F32) + two_ref[...].astype(F32)).astype(BF16)


def gather_kernel(owner_ref, part_ref, out_ref):
    for r in range(WIDE):
        source = owner_ref[r]
        total = part_ref[source, 0].astype(F32)
        for c in range(1, CHIPS):
            total = total + part_ref[source, c].astype(F32)
        out_ref[r * DRAFT : (r + 1) * DRAFT, :] = total.astype(BF16)


def swap(x):
    return lax.ppermute(x, "core", [(0, 1), (1, 0)])


def hop(x, distance):
    return lax.ppermute(x, "chip", [(c, c ^ distance) for c in range(CHIPS)])


def exchange(x, axes):
    return lax.all_to_all(x, axes, split_axis=0, concat_axis=0, tiled=True)


def local(
    hidden,
    norm_gain,
    w_query,
    w_keyval,
    query_gain,
    key_gain,
    cache_keys,
    cache_values,
    cache_lengths,
    owner_rank,
    draft_mask,
    w_output,
):
    tokens = WIDE * DRAFT
    piece = 2 * HD
    span = cache_keys.shape[1]
    shape = jax.ShapeDtypeStruct

    far = lambda x: pltpu.with_memory_space_constraint(x, pltpu.HBM)
    sent = pl.pallas_call(
        route_kernel,
        compiler_params=pltpu.CompilerParams(vmem_limit_bytes=4 * 1024 * 1024),
        out_shape=shape((WIDE, CHIPS, 40, HD), BF16),
        in_specs=[smem(), vmem(), vmem()],
        out_specs=vmem(),
    )(far(owner_rank), far(hidden), far(draft_mask))
    arrived = exchange(sent.reshape(WIDE * CHIPS, 40, HD), ("wide", "chip"))
    partner = swap(arrived)
    arrived = arrived.reshape(WIDE, CHIPS, 40, HD)
    partner = partner.reshape(WIDE, CHIPS, 40, HD)

    mine, piece_normed, marks = pl.pallas_call(
        query_kernel,
        compiler_params=pltpu.CompilerParams(vmem_limit_bytes=16 * 1024 * 1024),
        out_shape=(
            shape((WIDE * ROWS, HD), BF16),
            shape((tokens, piece), BF16),
            shape((WIDE, DRAFT // 2, HD), BF16),
        ),
        in_specs=[vmem()] * 2 + [anywhere()] * 3,
        out_specs=(vmem(),) * 3,
        scratch_shapes=[
            pltpu.VMEM((CHIPS * CORES * 2, HD), F32),
            pltpu.VMEM((CHIPS, CORES, piece, PER_HEAD * HD), BF16),
            pltpu.VMEM((1, HD), F32),
            pltpu.SemaphoreType.DMA((2 + CHIPS,)),
        ],
    )(
        arrived,
        partner,
        far(norm_gain.reshape(CHIPS * CORES * 2, HD)),
        far(w_query.reshape(CHIPS, CORES, piece, PER_HEAD * HD)),
        far(query_gain.reshape(1, HD)),
    )
    keyval = pl.pallas_call(
        keyval_kernel,
        compiler_params=pltpu.CompilerParams(vmem_limit_bytes=4 * 1024 * 1024),
        cost_estimate=pl.CostEstimate(flops=70000000, bytes_accessed=1200000, transcendentals=0),
        out_shape=shape((CHIPS, 2 * tokens, HD), BF16),
        in_specs=[vmem()] * 2,
        out_specs=vmem(),
    )(piece_normed, far(w_keyval))
    across = hop(mine, 4)
    near = [mine] + [hop(mine, d) for d in (1, 2, 3)]
    last = hop(across, 3)
    away = [across] + [hop(across, d) for d in (1, 2)] + [last]
    q_own = near + away
    q_other = [swap(x) for x in q_own[:5]]
    q_other.append(swap(q_own[5]))
    q_other += [swap(x) for x in q_own[6:]]
    kv_own = exchange(keyval, "chip")

    o_spec = pl.BlockSpec((CHIPS, ROWS, HD), lambda b: (0, b, 0))
    kv_spec = pl.BlockSpec((1, span, KVH * HD), lambda b: (b, 0, 0))
    attend = pl.pallas_call(
        attend_kernel,
        cost_estimate=pl.CostEstimate(
            flops=8 * WIDE * KVH * KVH * ROWS * span * HD,
            bytes_accessed=4 * WIDE * span * KVH * HD,
            transcendentals=WIDE * KVH * KVH * ROWS * span,
        ),
        compiler_params=pltpu.CompilerParams(vmem_limit_bytes=16 * 1024 * 1024),
        scratch_shapes=[
            pltpu.VMEM((2, KVH * ROWS, span), F32),
            pltpu.VMEM((2, KVH * ROWS, span), BF16),
            pltpu.VMEM((KVH, KVH * ROWS, HD), F32),
        ],
        out_shape=(
            shape((CHIPS, WIDE * ROWS, HD), BF16),
            shape((CHIPS, WIDE * ROWS, HD), BF16),
            shape((WIDE, 2 * KVH, HD), F32),
        ),
        grid=(WIDE,),
        in_specs=[smem()] + [vmem()] * (CHIPS * CORES) + [kv_spec] * 2,
        out_specs=(o_spec, o_spec, pl.BlockSpec((1, 2 * KVH, HD), lambda b: (b, 0, 0))),
    )
    o_own, o_other, lse = attend(
        cache_lengths, *q_own, *q_other, far(cache_keys), far(cache_values)
    )

    kv_other = swap(kv_own)
    joined = pl.pallas_call(
        join_kernel,
        compiler_params=pltpu.CompilerParams(vmem_limit_bytes=8 * 1024 * 1024),
        out_shape=shape((CHIPS, WIDE * ROWS + 2 * WIDE, HD), BF16),
        in_specs=[vmem()] * 4,
        out_specs=vmem(),
    )(o_own, swap(o_other), lse, swap(lse))
    parts = exchange(joined, "chip")

    drafted, draft_lse = pl.pallas_call(
        draft_kernel,
        compiler_params=pltpu.CompilerParams(vmem_limit_bytes=8 * 1024 * 1024),
        cost_estimate=pl.CostEstimate(
            flops=4000000000, bytes_accessed=2000000, transcendentals=70000
        ),
        out_shape=(shape((WIDE * ROWS, HD), F32),) * 2,
        in_specs=[vmem()] * 5,
        out_specs=(vmem(), vmem()),
    )(mine, far(kv_own), far(kv_other), key_gain.reshape(1, HD), marks)

    out_own, out_other = pl.pallas_call(
        finish_kernel,
        compiler_params=pltpu.CompilerParams(vmem_limit_bytes=16 * 1024 * 1024),
        out_shape=(shape((WIDE, CHIPS, DRAFT, piece), BF16),) * 2,
        in_specs=[vmem()] * 3 + [anywhere()],
        out_specs=(vmem(), vmem()),
        scratch_shapes=[
            pltpu.VMEM(w_output.shape, BF16),
            pltpu.SemaphoreType.DMA((CHIPS,)),
        ],
    )(parts, drafted, draft_lse, far(w_output))

    summed = pl.pallas_call(
        pair_kernel,
        compiler_params=pltpu.CompilerParams(vmem_limit_bytes=4 * 1024 * 1024),
        out_shape=shape((WIDE, CHIPS, DRAFT, piece), BF16),
        in_specs=[vmem()] * 2,
        out_specs=vmem(),
    )(out_own, swap(out_other))
    back = exchange(summed.reshape(WIDE * CHIPS, DRAFT, piece), ("wide", "chip"))
    return pl.pallas_call(
        gather_kernel,
        compiler_params=pltpu.CompilerParams(vmem_limit_bytes=4 * 1024 * 1024),
        out_shape=shape((tokens, piece), BF16),
        in_specs=[smem(), vmem()],
        out_specs=vmem(),
    )(owner_rank, back.reshape(WIDE, CHIPS, DRAFT, piece))


def solution(mesh):
    fine = Mesh(mesh.devices.reshape(WIDE, CHIPS, CORES), ("wide", "chip", "core"))
    narrow = ("chip", "core")
    in_specs = (
        P("wide", narrow),
        P(),
        P(None, narrow),
        P(narrow, None),
        P(),
        P(),
        P("wide", narrow, None),
        P("wide", narrow, None),
        P("wide"),
        P("wide"),
        P("wide", None, None),
        P(narrow, None),
    )
    out_specs = P("wide", narrow)

    return jax.shard_map(local, mesh=fine, in_specs=in_specs, out_specs=out_specs, check_vma=False)
```

```python
import math

import jax
import jax.numpy as jnp
from jax import lax
from jax.experimental import pallas as pl
from jax.experimental.pallas import tpu as pltpu
from jax.sharding import Mesh
from jax.sharding import PartitionSpec as P

HQ = 64
KVH = 4
HD = 128
DRAFT = 16
WIDE = 8
CHIPS = 8
CORES = 2
PER_HEAD = HQ // (CHIPS * CORES)
ROWS = PER_HEAD * DRAFT
TOGETHER = 2

EPS = 1e-06
DEAD = -1e30
LOG2E = 1.4426950408889634
SCALE2 = LOG2E / math.sqrt(HD)
F32 = jnp.float32
BF16 = jnp.bfloat16


def vmem():
    return pl.BlockSpec(memory_space=pltpu.VMEM)


def smem():
    return pl.BlockSpec(memory_space=pltpu.SMEM)


def anywhere():
    return pl.BlockSpec(memory_space=pl.ANY)


def rms(values, gain_row):
    mean = jnp.mean(values * values, axis=-1, keepdims=True)
    return values * lax.rsqrt(mean + EPS) * gain_row


def route_kernel(owner_ref, hidden_ref, mask_ref, out_ref):
    blank = jnp.zeros((DRAFT // 2, HD - 2 * DRAFT), F32)
    for r in range(WIDE):
        target = owner_ref[r]
        low = hidden_ref[r * DRAFT : (r + 1) * DRAFT, :HD]
        high = hidden_ref[r * DRAFT : (r + 1) * DRAFT, HD:]
        marks = mask_ref[r].astype(F32)
        marks = jnp.concatenate([marks[: DRAFT // 2], marks[DRAFT // 2 :], blank], axis=1)
        marks = marks.astype(BF16)
        for c in range(CHIPS):
            out_ref[target, c, 0:16, :] = low
            out_ref[target, c, 16:32, :] = high
            out_ref[target, c, 32:40, :] = marks


def features(ref, c):
    low = ref[:, c, 0:16, :].reshape(WIDE * DRAFT, HD)
    high = ref[:, c, 16:32, :].reshape(WIDE * DRAFT, HD)
    return jnp.concatenate([low, high], axis=1)


def query_kernel(
    own_ref,
    other_ref,
    gain_far,
    wq_far,
    qgain_far,
    mine_ref,
    slice_ref,
    marks_ref,
    gain_ref,
    wq_ref,
    qgain_ref,
    sem,
):
    gain_copy = pltpu.make_async_copy(gain_far, gain_ref, sem.at[0])
    qgain_copy = pltpu.make_async_copy(qgain_far, qgain_ref, sem.at[1])
    wq_copies = [
        pltpu.make_async_copy(wq_far.at[c], wq_ref.at[c], sem.at[2 + c]) for c in range(CHIPS)
    ]
    for copy in [gain_copy, qgain_copy] + wq_copies:
        copy.start()
    core = lax.axis_index("core")
    chip = lax.axis_index("chip")
    tokens = WIDE * DRAFT
    squares = jnp.zeros((tokens, 2 * HD), F32)
    for ref in (own_ref, other_ref):
        for c in range(CHIPS):
            block = features(ref, c).astype(F32)
            squares = squares + block * block
    width = CHIPS * CORES * 2 * HD
    scale = lax.rsqrt(jnp.sum(squares, axis=-1, keepdims=True) * (1.0 / width) + EPS)

    def normed(ref, c, side):
        block = features(ref, c).astype(F32)
        gain = gain_ref[pl.ds((c * CORES + side) * 2, 2), :]
        gain = jnp.concatenate([gain[0:1], gain[1:2]], axis=1)
        return (block * scale * gain).astype(BF16)

    gain_copy.wait()
    total = jnp.zeros((tokens, PER_HEAD * HD), F32)
    for c in range(CHIPS):
        wq_copies[c].wait()
        for ref, side in ((own_ref, core), (other_ref, 1 - core)):
            total = total + jnp.dot(
                normed(ref, c, side), wq_ref[c, side], preferred_element_type=F32
            )
    qgain_copy.wait()
    for j in range(PER_HEAD):
        head = rms(total[:, j * HD : (j + 1) * HD], qgain_ref[...]).astype(BF16)
        head = head.reshape(WIDE, DRAFT, HD)
        for b in range(WIDE):
            start = b * ROWS + j * DRAFT
            mine_ref[start : start + DRAFT, :] = head[b]
    for b in range(WIDE):
        marks_ref[b] = own_ref[b, 0, 32:40, :]
    slice_ref[...] = normed(own_ref, chip, core)


def keyval_kernel(slice_ref, wkv_ref, kv_ref):
    tokens = WIDE * DRAFT
    keyval = jnp.dot(slice_ref[...], wkv_ref[...], preferred_element_type=F32).astype(BF16)
    for c in range(CHIPS):
        kv = c // (CHIPS // KVH)
        kv_ref[c, 0:tokens, :] = keyval[:, kv * HD : (kv + 1) * HD]
        kv_ref[c, tokens : 2 * tokens, :] = keyval[:, (KVH + kv) * HD : (KVH + kv + 1) * HD]


def attend_kernel(length_ref, *refs):
    q_refs, refs = refs[: CHIPS * CORES], refs[CHIPS * CORES :]
    key_ref, value_ref, o_own_ref, o_other_ref, lse_ref, s_ref, p_ref, m_ref = refs
    step = pl.program_id(0)
    chip = lax.axis_index("chip")
    odd = lax.rem(chip, 2)
    span = key_ref.shape[1]
    tile = 2 * HD
    tiles = span // tile
    index = chip * CORES + lax.axis_index("core")
    ones = jnp.ones((span, HD), BF16)
    rows = lax.broadcasted_iota(jnp.int32, (HD, HD), 0)
    lanes = lax.broadcasted_iota(jnp.int32, (HD, HD), 1)

    def living(sub):
        return length_ref[step * TOGETHER + sub] - index * span

    def head(kv):
        return jnp.bitwise_xor(chip // 2, kv)

    def columns(kv):
        return pl.ds(pl.multiple_of(head(kv) * HD, HD), HD)

    def query(sub, kv):
        picked = [2 * kv, 2 * kv + 1, CHIPS + 2 * kv, CHIPS + 2 * kv + 1]
        here = pl.ds(pl.multiple_of((step * TOGETHER + sub) * ROWS, ROWS), ROWS)
        return jnp.concatenate([q_refs[i][here, :] for i in picked], axis=0)

    def score(u, sub, kv, i, q, top, live):
        at = slice(i * tile, (i + 1) * tile)
        keys = key_ref[sub, at, columns(kv)]
        part = lax.dot_general(q, keys, (((1,), (1,)), ((), ())), preferred_element_type=F32)
        if live is not None:
            place = lax.broadcasted_iota(jnp.int32, (1, tile), 1) + i * tile
            part = jnp.where(place < live, part, DEAD)
        s_ref[u % 2, :, at] = part
        high = jnp.maximum(part[:, :HD], part[:, HD:])
        return high if top is None else jnp.maximum(top, high)

    def close(u, top):
        m_ref[u % 4] = jnp.broadcast_to(jnp.max(top, axis=-1, keepdims=True), top.shape)

    def soft(u, i):
        count = KVH * ROWS // tiles
        at = slice(i * count, (i + 1) * count)
        top = m_ref[u % 4, at, :]
        for j in range(span // HD):
            part = s_ref[u % 2, at, j * HD : (j + 1) * HD]
            p_ref[u % 2, at, j * HD : (j + 1) * HD] = jnp.exp2((part - top) * SCALE2).astype(BF16)

    def value(u, sub, kv):
        values = jnp.concatenate([value_ref[sub, :, columns(kv)], ones], axis=1)
        summed = jnp.dot(p_ref[u % 2], values, preferred_element_type=F32)
        den = summed[:, HD:]
        out = (summed[:, :HD] / den).astype(BF16)
        here = pl.ds(pl.multiple_of(sub * ROWS, ROWS), ROWS)
        for i in range(2):
            target = jnp.bitwise_xor(chip, 2 * kv + i)
            o_own_ref[target, here, :] = out[i * ROWS : (i + 1) * ROWS]
            o_other_ref[target, here, :] = out[(2 + i) * ROWS : (3 + i) * ROWS]
        lse = m_ref[u % 4] * SCALE2 + jnp.log2(den)
        for side in range(2):
            block = lse[side * HD : (side + 1) * HD]
            line = jnp.sum(jnp.where(rows == lanes, block, 0.0), axis=0, keepdims=True)
            line = jnp.where(odd == 1, pltpu.roll(line, ROWS, 1), line)
            lse_ref[sub, pl.ds(side * KVH + head(kv), 1), :] = line

    def whole(units, live):
        count = len(units)
        for stage in range(count + 2):
            top = None
            q = query(*units[stage]) if stage < count else None
            if stage > 1:
                value(stage - 2, *units[stage - 2])
            for i in range(tiles):
                if stage < count:
                    top = score(stage, *units[stage], i, q, top, live)
                if 0 < stage <= count:
                    soft(stage - 1, i)
            if stage < count:
                close(stage, top)

    full = living(0) >= span
    for sub in range(1, TOGETHER):
        full = jnp.logical_and(full, living(sub) >= span)

    @pl.when(full)
    def _():
        whole([(sub, kv) for sub in range(TOGETHER) for kv in range(KVH)], None)

    @pl.when(jnp.logical_not(full))
    def _():
        @pl.loop(0, TOGETHER)
        def _(sub):
            live = living(sub)

            @pl.when(live <= 0)
            def _():
                here = pl.ds(pl.multiple_of(sub * ROWS, ROWS), ROWS)
                blank = jnp.zeros((ROWS, HD), BF16)
                for c in range(CHIPS):
                    o_own_ref[c, here, :] = blank
                    o_other_ref[c, here, :] = blank
                lse_ref[sub] = jnp.full((2 * KVH, HD), DEAD, F32)

            @pl.when(live > 0)
            def _():
                whole([(sub, kv) for kv in range(KVH)], live)


def join_kernel(mine_ref, theirs_ref, lse_ref, lse_in_ref, out_ref):
    one = lse_ref[:, 0:KVH, :].reshape(WIDE * KVH, HD)
    two = lse_in_ref[:, KVH : 2 * KVH, :].reshape(WIDE * KVH, HD)
    top = jnp.maximum(one, two)
    weight_one = jnp.exp2(one - top)
    weight_two = jnp.exp2(two - top)
    den = weight_one + weight_two
    lse = (top + jnp.log2(den)).reshape(WIDE, KVH, HD)
    shares = jnp.concatenate(
        [weight_one / den, weight_two / den, jnp.zeros((2 * WIDE * KVH, HD), F32)], axis=0
    )
    shares = shares.T
    for b in range(WIDE):
        for kv in range(KVH):
            j = b * KVH + kv
            col_one = shares[:, j : j + 1]
            col_two = shares[:, WIDE * KVH + j : WIDE * KVH + j + 1]
            for p in range(2):
                c = 2 * kv + p
                at = slice(b * ROWS, (b + 1) * ROWS)
                part = slice(p * ROWS, (p + 1) * ROWS)
                mixed = (
                    mine_ref[c, at, :].astype(F32) * col_one[part]
                    + theirs_ref[c, at, :].astype(F32) * col_two[part]
                )
                out_ref[c, at, :] = mixed.astype(BF16)
    lanes = lax.broadcasted_iota(jnp.int32, (WIDE, HD), 1)
    for kv in range(KVH):
        line = lse[:, kv, :]
        first = line.astype(BF16).astype(F32)
        rest = line - first
        second = rest.astype(BF16).astype(F32)
        third = (rest - second).astype(BF16).astype(F32)
        turned = [pltpu.roll(x, ROWS, 1) for x in (first, second, third)]
        for p in range(2):
            a = first if p == 0 else turned[0]
            m = turned[1] if p == 0 else second
            z = third if p == 0 else turned[2]
            base = WIDE * ROWS
            tail = jnp.concatenate(
                [jnp.where(lanes < ROWS, a, m), jnp.where(lanes < ROWS, z, 0.0)], axis=0
            )
            out_ref[2 * kv + p, base : base + 2 * WIDE, :] = tail.astype(BF16)


def draft_kernel(q_ref, kv_own_ref, kv_other_ref, kgain_ref, mask_ref, out_ref, lse_ref):
    tokens = WIDE * DRAFT
    total = jnp.zeros((2 * tokens, HD), F32)
    for ref in (kv_own_ref, kv_other_ref):
        for c in range(CHIPS):
            total = total + ref[c].astype(F32)
    keys = rms(total[:tokens], kgain_ref[...]).astype(BF16)
    values = total[tokens:].astype(BF16)
    lanes = lax.broadcasted_iota(jnp.int32, (DRAFT, HD), 1)
    for b in range(WIDE):
        at = slice(b * ROWS, (b + 1) * ROWS)
        marks = mask_ref[b].astype(F32)
        late = pltpu.roll(marks, HD - DRAFT, 1)
        marks = jnp.concatenate([marks, late], axis=0)
        marks = jnp.where(lanes < DRAFT, marks, 0.0)
        if b:
            marks = pltpu.roll(marks, b * DRAFT, 1)
        allowed = jnp.concatenate([marks] * PER_HEAD, axis=0) > 0.5
        scores = lax.dot_general(
            q_ref[at, :], keys, (((1,), (1,)), ((), ())), preferred_element_type=F32
        )
        scores = jnp.where(allowed, scores, DEAD)
        top = jnp.max(scores, axis=-1, keepdims=True)
        weights = jnp.exp2((scores - top) * SCALE2)
        den = jnp.sum(weights, axis=-1, keepdims=True)
        summed = jnp.dot(weights.astype(BF16), values, preferred_element_type=F32)
        out_ref[at, :] = summed / den
        lse_ref[at, :] = jnp.broadcast_to(top * SCALE2 + jnp.log2(den), (ROWS, HD))


def finish_kernel(
    part_ref, draft_ref, lse_ref, wo_far, out_own_ref, out_other_ref, wo_ref, sem
):
    core = lax.axis_index("core")
    tokens = WIDE * DRAFT
    wo_copies = []
    for c in range(CHIPS):
        columns = pl.ds(c * CORES * 2 * HD, CORES * 2 * HD)
        wo_copies.append(
            pltpu.make_async_copy(wo_far.at[:, columns], wo_ref.at[:, columns], sem.at[c])
        )
        wo_copies[c].start()
    base = WIDE * ROWS
    lines = []
    for c in range(CHIPS):
        head = part_ref[c, base : base + WIDE, :].astype(F32)
        tail = part_ref[c, base + WIDE : base + 2 * WIDE, :].astype(F32)
        lines.append(head + pltpu.roll(head, ROWS, 1) + tail)
    columns = jnp.concatenate(lines + [jnp.zeros((HD - CHIPS * WIDE, HD), F32)], axis=0).T
    attended = []
    for b in range(WIDE):
        at = slice(b * ROWS, (b + 1) * ROWS)
        cols = [columns[0:ROWS, c * WIDE + b : c * WIDE + b + 1] for c in range(CHIPS)]
        cols = [jnp.broadcast_to(col, (ROWS, HD)) for col in cols]
        draft = lse_ref[at, :]
        peak = draft
        for col in cols:
            peak = jnp.maximum(peak, col)
        share = jnp.exp2(draft - peak)
        numer = draft_ref[at, :] * share
        denom = share
        for c in range(CHIPS):
            share = jnp.exp2(cols[c] - peak)
            numer = numer + part_ref[c, at, :].astype(F32) * share
            denom = denom + share
        attended.append((numer / denom).astype(BF16))
    attended = jnp.stack(attended, axis=0)
    rows = jnp.concatenate(
        [
            attended[:, j * DRAFT : (j + 1) * DRAFT, :].reshape(tokens, HD)
            for j in range(PER_HEAD)
        ],
        axis=1,
    )
    piece = 2 * HD
    for c in range(CHIPS):
        wo_copies[c].wait()
        for ref, side in ((out_own_ref, core), (out_other_ref, 1 - core)):
            column = pl.multiple_of((c * CORES + side) * piece, piece)
            out = jnp.dot(rows, wo_ref[:, pl.ds(column, piece)], preferred_element_type=F32)
            ref[:, c] = out.astype(BF16).reshape(WIDE, DRAFT, piece)


def pair_kernel(one_ref, two_ref, out_ref):
    out_ref[...] = (one_ref[...].astype(F32) + two_ref[...].astype(F32)).astype(BF16)


def gather_kernel(owner_ref, part_ref, out_ref):
    for r in range(WIDE):
        source = owner_ref[r]
        total = part_ref[source, 0].astype(F32)
        for c in range(1, CHIPS):
            total = total + part_ref[source, c].astype(F32)
        out_ref[r * DRAFT : (r + 1) * DRAFT, :] = total.astype(BF16)


def swap(x):
    return lax.ppermute(x, "core", [(0, 1), (1, 0)])


def hop(x, distance):
    return lax.ppermute(x, "chip", [(c, c ^ distance) for c in range(CHIPS)])


def exchange(x, axes):
    return lax.all_to_all(x, axes, split_axis=0, concat_axis=0, tiled=True)


def local(
    hidden,
    norm_gain,
    w_query,
    w_keyval,
    query_gain,
    key_gain,
    cache_keys,
    cache_values,
    cache_lengths,
    owner_rank,
    draft_mask,
    w_output,
):
    tokens = WIDE * DRAFT
    piece = 2 * HD
    span = cache_keys.shape[1]
    shape = jax.ShapeDtypeStruct

    far = lambda x: pltpu.with_memory_space_constraint(x, pltpu.HBM)
    sent = pl.pallas_call(
        route_kernel,
        compiler_params=pltpu.CompilerParams(vmem_limit_bytes=4 * 1024 * 1024),
        out_shape=shape((WIDE, CHIPS, 40, HD), BF16),
        in_specs=[smem(), vmem(), vmem()],
        out_specs=vmem(),
    )(far(owner_rank), far(hidden), far(draft_mask))
    arrived = exchange(sent.reshape(WIDE * CHIPS, 40, HD), ("wide", "chip"))
    partner = swap(arrived)
    arrived = arrived.reshape(WIDE, CHIPS, 40, HD)
    partner = partner.reshape(WIDE, CHIPS, 40, HD)

    mine, piece_normed, marks = pl.pallas_call(
        query_kernel,
        compiler_params=pltpu.CompilerParams(vmem_limit_bytes=16 * 1024 * 1024),
        out_shape=(
            shape((WIDE * ROWS, HD), BF16),
            shape((tokens, piece), BF16),
            shape((WIDE, DRAFT // 2, HD), BF16),
        ),
        in_specs=[vmem()] * 2 + [anywhere()] * 3,
        out_specs=(vmem(),) * 3,
        scratch_shapes=[
            pltpu.VMEM((CHIPS * CORES * 2, HD), F32),
            pltpu.VMEM((CHIPS, CORES, piece, PER_HEAD * HD), BF16),
            pltpu.VMEM((1, HD), F32),
            pltpu.SemaphoreType.DMA((2 + CHIPS,)),
        ],
    )(
        arrived,
        partner,
        far(norm_gain.reshape(CHIPS * CORES * 2, HD)),
        far(w_query.reshape(CHIPS, CORES, piece, PER_HEAD * HD)),
        far(query_gain.reshape(1, HD)),
    )
    keyval = pl.pallas_call(
        keyval_kernel,
        compiler_params=pltpu.CompilerParams(vmem_limit_bytes=4 * 1024 * 1024),
        cost_estimate=pl.CostEstimate(flops=70000000, bytes_accessed=1200000, transcendentals=0),
        out_shape=shape((CHIPS, 2 * tokens, HD), BF16),
        in_specs=[vmem()] * 2,
        out_specs=vmem(),
    )(piece_normed, far(w_keyval))
    across = hop(mine, 4)
    near = [mine] + [hop(mine, d) for d in (1, 2, 3)]
    last = hop(across, 3)
    away = [across] + [hop(across, d) for d in (1, 2)] + [last]
    q_own = near + away
    q_other = [swap(x) for x in q_own[:5]]
    q_other.append(swap(q_own[5]))
    q_other += [swap(x) for x in q_own[6:]]
    kv_own = exchange(keyval, "chip")

    o_spec = pl.BlockSpec((CHIPS, TOGETHER * ROWS, HD), lambda b: (0, b, 0))
    kv_spec = pl.BlockSpec((TOGETHER, span, KVH * HD), lambda b: (b, 0, 0))
    attend = pl.pallas_call(
        attend_kernel,
        cost_estimate=pl.CostEstimate(
            flops=8 * WIDE * KVH * KVH * ROWS * span * HD,
            bytes_accessed=4 * WIDE * span * KVH * HD,
            transcendentals=WIDE * KVH * KVH * ROWS * span,
        ),
        compiler_params=pltpu.CompilerParams(vmem_limit_bytes=18 * 1024 * 1024),
        scratch_shapes=[
            pltpu.VMEM((2, KVH * ROWS, span), F32),
            pltpu.VMEM((2, KVH * ROWS, span), BF16),
            pltpu.VMEM((KVH, KVH * ROWS, HD), F32),
        ],
        out_shape=(
            shape((CHIPS, WIDE * ROWS, HD), BF16),
            shape((CHIPS, WIDE * ROWS, HD), BF16),
            shape((WIDE, 2 * KVH, HD), F32),
        ),
        grid=(WIDE // TOGETHER,),
        in_specs=[smem()] + [vmem()] * (CHIPS * CORES) + [kv_spec] * 2,
        out_specs=(o_spec, o_spec, pl.BlockSpec((TOGETHER, 2 * KVH, HD), lambda b: (b, 0, 0))),
    )
    o_own, o_other, lse = attend(
        cache_lengths, *q_own, *q_other, far(cache_keys), far(cache_values)
    )

    kv_other = swap(kv_own)
    joined = pl.pallas_call(
        join_kernel,
        compiler_params=pltpu.CompilerParams(vmem_limit_bytes=8 * 1024 * 1024),
        out_shape=shape((CHIPS, WIDE * ROWS + 2 * WIDE, HD), BF16),
        in_specs=[vmem()] * 4,
        out_specs=vmem(),
    )(o_own, swap(o_other), lse, swap(lse))
    parts = exchange(joined, "chip")

    drafted, draft_lse = pl.pallas_call(
        draft_kernel,
        compiler_params=pltpu.CompilerParams(vmem_limit_bytes=8 * 1024 * 1024),
        cost_estimate=pl.CostEstimate(
            flops=4000000000, bytes_accessed=2000000, transcendentals=70000
        ),
        out_shape=(shape((WIDE * ROWS, HD), F32),) * 2,
        in_specs=[vmem()] * 5,
        out_specs=(vmem(), vmem()),
    )(mine, far(kv_own), far(kv_other), key_gain.reshape(1, HD), marks)

    out_own, out_other = pl.pallas_call(
        finish_kernel,
        compiler_params=pltpu.CompilerParams(vmem_limit_bytes=16 * 1024 * 1024),
        out_shape=(shape((WIDE, CHIPS, DRAFT, piece), BF16),) * 2,
        in_specs=[vmem()] * 3 + [anywhere()],
        out_specs=(vmem(), vmem()),
        scratch_shapes=[
            pltpu.VMEM(w_output.shape, BF16),
            pltpu.SemaphoreType.DMA((CHIPS,)),
        ],
    )(parts, drafted, draft_lse, far(w_output))

    summed = pl.pallas_call(
        pair_kernel,
        compiler_params=pltpu.CompilerParams(vmem_limit_bytes=4 * 1024 * 1024),
        out_shape=shape((WIDE, CHIPS, DRAFT, piece), BF16),
        in_specs=[vmem()] * 2,
        out_specs=vmem(),
    )(out_own, swap(out_other))
    back = exchange(summed.reshape(WIDE * CHIPS, DRAFT, piece), ("wide", "chip"))
    return pl.pallas_call(
        gather_kernel,
        compiler_params=pltpu.CompilerParams(vmem_limit_bytes=4 * 1024 * 1024),
        out_shape=shape((tokens, piece), BF16),
        in_specs=[smem(), vmem()],
        out_specs=vmem(),
    )(owner_rank, back.reshape(WIDE, CHIPS, DRAFT, piece))


def solution(mesh):
    fine = Mesh(mesh.devices.reshape(WIDE, CHIPS, CORES), ("wide", "chip", "core"))
    narrow = ("chip", "core")
    in_specs = (
        P("wide", narrow),
        P(),
        P(None, narrow),
        P(narrow, None),
        P(),
        P(),
        P("wide", narrow, None),
        P("wide", narrow, None),
        P("wide"),
        P("wide"),
        P("wide", None, None),
        P(narrow, None),
    )
    out_specs = P("wide", narrow)

    return jax.shard_map(local, mesh=fine, in_specs=in_specs, out_specs=out_specs, check_vma=False)
```
